256 devices in a mesh: pair: 4 (over y_lo, core), col: 64 (over y_hi, x, z).
Axes of the slice: x: 4, y: 4 (y_hi: 2, y_lo: 2; y = y_hi * 2 + y_lo), z: 8, core: 2. Of those that a mesh axis runs over, the one named last changes fastest.
Arguments:
- amplitudes: bfloat16 [1536, 4096], P('pair', 'col'), may hold values from -6 to 6
- integrals: bfloat16 [4096, 81920], P('pair', 'col'), may hold values from -0.25 to 0.25
- irrep_start: int32 [9], replicated, may hold values from 0 to 4096, as said below
- pair_irrep: int32 [1536], P('pair'), may hold values from 0 to 7
Outputs:
- ladder: bfloat16 [1536, 81920], P('pair', 'col')
The draws below stay inside these ranges and needn't reach their ends.
Inputs may be any that keep to these rules, and one draw needn't show every extreme that they name: Strictly rising multiples of 128; the first is 0 and the last is 4096; irrep j owns rows irrep_start[j] to irrep_start[j+1] - 1.
All inputs are finite; a program needn't handle non-finite values.
Results may differ from the reference program's by a relative error of at most 0.001.
Values may be sent and summed in bfloat16 or wider, within the bound.
A program may use at most 64 MiB of HBM per device.

```python
import jax
import jax.numpy as jnp

K = 4096
PAIRS = 1536
COLS = 81920


def draw_irrep_start(key, part):
    order = jax.random.permutation(key, 31) + 1
    cuts = jnp.sort(order[:7]).astype(jnp.int32) * (K // 32)
    head = jnp.zeros((1,), jnp.int32)
    tail = jnp.full((1,), K, jnp.int32)
    return jnp.concatenate([head, cuts, tail]).astype(jnp.int32)


def set_ends(result, stream_key, smallest, largest):
    place = [jax.random.randint(jax.random.fold_in(stream_key, axis), (), 0, length) for axis, length in enumerate(result.shape)]
    widest = result.shape.index(max(result.shape))
    next_to = place[:widest] + [(place[widest] + 1) % result.shape[widest]] + place[widest + 1:]
    return result.at[tuple(place)].set(smallest).at[tuple(next_to)].set(largest)


def shard_levels(stream_key, shape, split, least, top_value):
    level, own = 1.0, jax.random.fold_in(stream_key, 6)
    for position, blocks in split:
        steps = jnp.exp(jax.random.uniform(jax.random.fold_in(own, position), (blocks,), jnp.float32, least / len(split), top_value / len(split)))
        level = level * jnp.repeat(steps, shape[position] // blocks).reshape([-1 if axis == position else 1 for axis in range(len(shape))])
    return level


def scatter_about(rng, shape, spread, most, shards=(), held_as=jnp.bfloat16):
    level = shard_levels(rng, shape, shards, -0.22, 0.18) if shards else 1.0
    array = jax.random.normal(rng, shape, jnp.float32) * spread * level
    return jnp.minimum(jnp.maximum(array, -most), most).astype(held_as)


def setup_inputs(seed: int = 0) -> dict:
    keys = jax.random.split(jax.random.key(seed), 5)
    amplitudes = scatter_about(keys[0], (PAIRS, K), 1.0, 6.0, ((0, 4), (1, 64)))
    integrals = scatter_about(keys[1], (K, COLS), (K // 8) ** -0.5, 0.25, ((0, 4), (1, 64)))
    irrep_start = draw_irrep_start(jax.random.fold_in(keys[4], 71), 0)
    pair_irrep = set_ends(jax.random.randint(keys[3], (PAIRS,), 0, 8), jax.random.fold_in(keys[3], 1), 0, 7).astype(jnp.int32)
    return dict(amplitudes=amplitudes, integrals=integrals, irrep_start=irrep_start, pair_irrep=pair_irrep)


def reference(amplitudes, integrals, irrep_start, pair_irrep):
    rows = jnp.arange(K, dtype=jnp.int32)
    row_irrep = jnp.sum((rows[:, None] >= irrep_start[None, 1:8]).astype(jnp.int32), axis=1)
    keep = pair_irrep[:, None] == row_irrep[None, :]
    masked = jnp.where(keep, amplitudes, jnp.zeros_like(amplitudes))
    return jnp.dot(masked, integrals, preferred_element_type=jnp.float32).astype(jnp.bfloat16)
```

```python
import functools

import jax
import jax.numpy as jnp
from jax import lax
from jax.experimental import pallas as pl
from jax.experimental.pallas import tpu as pltpu
from jax.sharding import PartitionSpec as P

MESH = pl.DeviceIdType.MESH
NX, NZ = 4, 8
TILE = 256
F32 = jnp.float32


def iota(shape, axis):
    return lax.broadcasted_iota(jnp.int32, shape, axis)


def kernel(
    cap, slots,
    start_ref, irr_ref, amp_ref, int_ref,
    out_ref, flag_ref,
    irr_all, comp, gat, ints, pick, lhs, own, mix, low, acc, sendb, recvb,
    irr_send, irr_recv, yx_send, yx_recv, z_send, z_recv, int_send, int_recv, own_sem, ex_send, ex_recv,
):
    pairs = irr_ref.shape[1]
    depth, cols = int_ref.shape
    rows = amp_ref.shape[0]
    half = 2 * depth
    tiles = cols // TILE

    pair = lax.axis_index("pair")
    col = lax.axis_index("col")
    h, core = pair // 2, pair % 2
    yh, x, z = col // (NX * NZ), (col // NZ) % NX, col % NZ
    kind = (h == yh).astype(jnp.int32)
    selfish = h == yh

    def at(hh, cc, yy, xx, zz):
        return (hh * 2 + cc, (yy * NX + xx) * NZ + zz)

    def signal(dev):
        pl.semaphore_signal(barrier, inc=1, device_id=dev, device_id_type=MESH)

    barrier = pltpu.get_barrier_semaphore()
    relations = ((0, 1), (1, 0), (1, 1))
    for dh, dc in relations:
        signal(at((h + dh) % 2, (core + dc) % 2, yh, x, z))
    signal(at(h, core, yh, x, (z + 1) % NZ))
    signal(at(h, core, yh, x, (z + NZ - 1) % NZ))
    for u in range(2):
        for dx in range(NX):
            source = at(u, core, h, (x + dx) % NX, z)
            if dx == 0:
                @pl.when(jnp.logical_not(jnp.logical_and(selfish, u == h)))
                def _(source=source):
                    signal(source)
            else:
                signal(source)

    own_copy = pltpu.make_async_copy(int_ref, ints.at[pl.ds(core * depth, depth)], own_sem)
    own_copy.start()

    def row_irrep(row):
        total = jnp.int32(0)
        for j in range(1, 8):
            total = total + (row >= start_ref[j]).astype(jnp.int32)
        return total

    eye = iota((pairs, pairs), 0) == iota((pairs, pairs), 1)
    below = iota((pairs, pairs), 1) < iota((pairs, pairs), 0)
    above = iota((pairs, pairs), 0) < iota((pairs, pairs), 1)

    def down(v):
        return jnp.sum(jnp.where(eye, v, 0.0), axis=1, keepdims=True)

    def touch(v, which):
        total = jnp.zeros_like(v)
        for r in range(8):
            meets = jnp.logical_and(start_ref[r] < half * (which + 1), start_ref[r + 1] > half * which)
            total = total + jnp.where(v == float(r), jnp.where(meets, 1.0, 0.0), 0.0)
        return total

    mine_l = irr_ref[...].astype(F32)
    mine_s = down(mine_l)
    rank_s = jnp.sum(jnp.where(jnp.logical_and(below, mine_s == mine_l), 1.0, 0.0), axis=1, keepdims=True)
    here = row_irrep(col * rows).astype(F32)
    where_s = jnp.where(mine_s == here, rank_s, -1.0)
    chosen = jnp.where(where_s == iota((pairs, cap), 1).astype(F32), 1.0, 0.0).astype(jnp.bfloat16)
    block = jnp.dot(amp_ref[...], chosen, preferred_element_type=F32).astype(jnp.bfloat16)
    comp[...] = block

    @pl.when(selfish)
    def _():
        gat[1, z, x] = block

    pick_own = (mine_s * 512.0 + rank_s).astype(jnp.int32) - iota((pairs, cap), 1)

    n_targets = 5 + 2 * NX - kind
    pl.semaphore_wait(barrier, n_targets)

    def yx_copy(u, dx):
        return pltpu.make_async_remote_copy(
            src_ref=comp, dst_ref=gat.at[kind, z, x],
            send_sem=yx_send.at[u * NX + dx], recv_sem=yx_recv.at[kind, x],
            device_id=at(yh, core, u, (x + dx) % NX, z), device_id_type=MESH,
        )

    def not_self(u, dx, act):
        if dx == 0:
            @pl.when(jnp.logical_not(jnp.logical_and(selfish, u == yh)))
            def _():
                act()
        else:
            act()

    for dx in (2, 1, 3, 0):
        for u in range(2):
            not_self(u, dx, lambda u=u, dx=dx: yx_copy(u, dx).start())

    def irr_copy(k):
        dh, dc = relations[k]
        return pltpu.make_async_remote_copy(
            src_ref=irr_ref, dst_ref=irr_all.at[pair],
            send_sem=irr_send.at[k], recv_sem=irr_recv.at[k],
            device_id=at((h + dh) % 2, (core + dc) % 2, yh, x, z), device_id_type=MESH,
        )

    for k in range(3):
        irr_copy(k).start()

    int_copy = pltpu.make_async_remote_copy(
        src_ref=int_ref, dst_ref=ints.at[pl.ds(core * depth, depth)],
        send_sem=int_send, recv_sem=int_recv,
        device_id=at(h, 1 - core, yh, x, z), device_id_type=MESH,
    )
    int_copy.start()

    def z_copy(t, d, s, q):
        step = 1 if d == 0 else NZ - 1
        slab = (z + NZ * NZ - (s - 1) * step) % NZ
        piece = gat.at[t, slab, pl.ds(2 * q, 2)]
        return pltpu.make_async_remote_copy(
            src_ref=piece, dst_ref=piece,
            send_sem=z_send.at[t, d, s - 1, q], recv_sem=z_recv.at[t, d, s - 1, q],
            device_id=at(h, core, yh, x, (z + step) % NZ), device_id_type=MESH,
        )

    def z_arrival(t, d, s, q):
        step = 1 if d == 0 else NZ - 1
        slab = (z + NZ * NZ - s * step) % NZ
        piece = gat.at[t, slab, pl.ds(2 * q, 2)]
        return pltpu.make_async_remote_copy(
            src_ref=piece, dst_ref=piece,
            send_sem=z_send.at[t, d, s - 1, q], recv_sem=z_recv.at[t, d, s - 1, q],
            device_id=at(h, core, yh, x, (z + step) % NZ), device_id_type=MESH,
        )

    z_steps = [(s, d, q) for s in range(1, 5) for q in range(2) for d in range(2) if s < 4 or q == d]

    def gather_start(t):
        for dx in range(NX):
            xx = (x + dx) % NX
            arrival = pltpu.make_async_remote_copy(
                src_ref=comp, dst_ref=gat.at[t, z, xx],
                send_sem=yx_send.at[0], recv_sem=yx_recv.at[t, xx],
                device_id=at(h, core, yh, xx, z), device_id_type=MESH,
            )
            if t == 1 and dx == 0:
                @pl.when(jnp.logical_not(selfish))
                def _(arrival=arrival):
                    arrival.wait_recv()
            else:
                arrival.wait_recv()
        for s, d, q in z_steps:
            if s == 1:
                z_copy(t, d, 1, q).start()

    def gather_rest(t):
        for s, d, q in z_steps:
            if s > 1:
                z_arrival(t, d, s - 1, q).wait_recv()
                z_copy(t, d, s, q).start()
        for s, d, q in z_steps:
            if (s + 1, d, q) not in z_steps:
                z_arrival(t, d, s, q).wait_recv()

    gather_start(0)

    for k in range(3):
        dh, dc = relations[k]
        arrival = pltpu.make_async_remote_copy(
            src_ref=irr_ref, dst_ref=irr_all.at[((h + dh) % 2) * 2 + (core + dc) % 2],
            send_sem=irr_send.at[k], recv_sem=irr_recv.at[k],
            device_id=at((h + dh) % 2, (core + dc) % 2, yh, x, z), device_id_type=MESH,
        )
        arrival.wait_recv()

    theirs_l = irr_all[(1 - h) * 2 + core].astype(F32)
    theirs_s = down(theirs_l)
    rank_l = jnp.sum(jnp.where(jnp.logical_and(above, theirs_s == theirs_l), 1.0, 0.0), axis=0, keepdims=True)
    key_l = theirs_l * 512.0 + rank_l + 1.0
    src_l = touch(theirs_l, h)
    both_l = src_l * touch(theirs_l, 1 - h)
    src_s, both_s = down(src_l), down(both_l)
    pos1 = jnp.sum(jnp.where(above, src_s, 0.0), axis=0, keepdims=True)
    pos2 = jnp.sum(src_l, axis=1, keepdims=True) + jnp.sum(jnp.where(above, both_s, 0.0), axis=0, keepdims=True)
    pos1 = jnp.where(src_l > 0.0, pos1, -1.0)
    pos2 = jnp.where(both_l > 0.0, pos2, -1.0)
    slot = iota((slots, pairs), 0).astype(F32)
    is_low = pos2 == slot
    key_slot = jnp.sum(jnp.where(jnp.logical_or(pos1 == slot, is_low), key_l, 0.0), axis=1, keepdims=True)
    low[...] = jnp.sum(jnp.where(is_low, 1.0, 0.0), axis=1, keepdims=True)
    pick[...] = (key_slot - 1.0).astype(jnp.int32) - iota((slots, cap), 1)

    gather_rest(0)

    def expand(t, keys, dst):
        for b in range(half // 128):
            here = row_irrep(h * half + b * 128) * 512
            one_hot = jnp.where(keys == here, 1.0, 0.0).astype(jnp.bfloat16)
            zz, xx = 2 * (b % (NZ // 2)), b // (NZ // 2)
            packed = jnp.concatenate([gat[t, zz, xx], gat[t, zz + 1, xx]], axis=0)
            part = lax.dot_general(one_hot, packed, (((1,), (1,)), ((), ())), preferred_element_type=F32)
            dst[:, pl.ds(b * 128, 128)] = part.astype(jnp.bfloat16)

    expand(0, pick[...], lhs)
    own_copy.wait()
    int_copy.wait_recv()

    def ex_copy(j):
        return pltpu.make_async_remote_copy(
            src_ref=sendb.at[j], dst_ref=recvb.at[j],
            send_sem=ex_send.at[j], recv_sem=ex_recv.at[j],
            device_id=at(1 - h, core, yh, x, z), device_id_type=MESH,
        )

    @pl.loop(0, tiles + 1)
    def _(j):
        @pl.when(j < tiles)
        def _():
            part = jnp.dot(lhs[...], ints[:, pl.ds(pl.multiple_of(j * TILE, TILE), TILE)], preferred_element_type=F32)
            high = part.astype(jnp.bfloat16).astype(F32)
            sendb[j] = jnp.where(low[...] > 0.0, part - high, part).astype(jnp.bfloat16)

        @pl.when(j > 0)
        def _():
            ex_copy(j - 1).start()

    gather_start(1)
    src_l = touch(mine_l, 1 - h)
    both_l = src_l * touch(mine_l, h)
    src_s, both_s = down(src_l), down(both_l)
    pos1 = jnp.sum(jnp.where(below, src_l, 0.0), axis=1, keepdims=True)
    pos2 = jnp.sum(src_l, axis=1, keepdims=True) + jnp.sum(jnp.where(below, both_l, 0.0), axis=1, keepdims=True)
    pos1 = jnp.where(src_s > 0.0, pos1, -1.0)
    pos2 = jnp.where(both_s > 0.0, pos2, -1.0)
    slot = iota((pairs, slots), 1).astype(F32)
    mix[...] = jnp.where(jnp.logical_or(pos1 == slot, pos2 == slot), 1.0, 0.0).astype(jnp.bfloat16)

    fits = jnp.ones((1, 1), F32)
    for g in range(4):
        v = jnp.where(pair == g, mine_l, irr_all[g].astype(F32))
        for r in range(8):
            count = jnp.sum(jnp.where(v == float(r), 1.0, 0.0), axis=1, keepdims=True)
            fits = jnp.where(count > float(cap), 0.0, fits)
        src = touch(v, 1 - g // 2)
        need = jnp.sum(src + src * touch(v, g // 2), axis=1, keepdims=True)
        fits = jnp.where(need > float(slots), 0.0, fits)
    flag_ref[...] = jnp.broadcast_to(fits, flag_ref.shape)

    gather_rest(1)
    expand(1, pick_own, own)

    @pl.loop(0, tiles)
    def _(j):
        acc[j] = jnp.dot(own[...], ints[:, pl.ds(pl.multiple_of(j * TILE, TILE), TILE)], preferred_element_type=F32)

    @pl.loop(0, tiles)
    def _(j):
        ex_copy(j).wait_recv()
        total = acc[j] + jnp.dot(mix[...], recvb[j], preferred_element_type=F32)
        out_ref[:, pl.ds(pl.multiple_of(j * TILE, TILE), TILE)] = total.astype(jnp.bfloat16)

    for dx in range(NX):
        for u in range(2):
            not_self(u, dx, lambda u=u, dx=dx: yx_copy(u, dx).wait_send())
    for k in range(3):
        irr_copy(k).wait_send()
    int_copy.wait_send()
    for t in range(2):
        for s, d, q in z_steps:
            z_copy(t, d, s, q).wait_send()

    @pl.loop(0, tiles)
    def _(j):
        ex_copy(j).wait_send()


def ladder(cap, slots, collective_id, starts, irreps, amp, integrals):
    rows, pairs = amp.shape
    depth, cols = integrals.shape
    half, tiles = 2 * depth, cols // TILE
    bf16 = jnp.bfloat16
    dma = pltpu.SemaphoreType.DMA
    vmem = pl.BlockSpec(memory_space=pltpu.VMEM)
    return pl.pallas_call(
        functools.partial(kernel, cap, slots),
        out_shape=(jax.ShapeDtypeStruct((pairs, cols), bf16), jax.ShapeDtypeStruct((8, 128), F32)),
        in_specs=[pl.BlockSpec(memory_space=pltpu.SMEM), vmem, vmem, pl.BlockSpec(memory_space=pl.ANY)],
        out_specs=(vmem, vmem),
        scratch_shapes=[
            pltpu.VMEM((4, 1, pairs), jnp.int32),
            pltpu.VMEM((rows, cap), bf16),
            pltpu.VMEM((2, NZ, NX, rows, cap), bf16),
            pltpu.VMEM((half, cols), bf16),
            pltpu.VMEM((slots, cap), jnp.int32),
            pltpu.VMEM((slots, half), bf16),
            pltpu.VMEM((pairs, half), bf16),
            pltpu.VMEM((pairs, slots), bf16),
            pltpu.VMEM((slots, 1), F32),
            pltpu.VMEM((tiles, pairs, TILE), F32),
            pltpu.VMEM((tiles, slots, TILE), bf16),
            pltpu.VMEM((tiles, slots, TILE), bf16),
            dma((3,)), dma((3,)), dma((2 * NX,)), dma((2, NX)), dma((2, 2, 4, 2)), dma((2, 2, 4, 2)),
            dma, dma, dma, dma((tiles,)), dma((tiles,)),
        ],
        compiler_params=pltpu.CompilerParams(
            collective_id=collective_id, has_side_effects=True, vmem_limit_bytes=56 * 1024 * 1024
        ),
        name="ladder_" + str(slots),
    )(starts, irreps, amp, integrals)


def per_device(amplitudes, integrals, irrep_start, pair_irrep):
    pairs = amplitudes.shape[0]
    operands = (irrep_start, pair_irrep.reshape(1, pairs), amplitudes.T, integrals)
    out, fits = ladder(128, 448, 0, *operands)
    return lax.cond(
        fits[0, 0] > 0.0,
        lambda *_: out,
        lambda *args: ladder(pairs, 2 * pairs, 1, *args)[0],
        *operands,
    )


def solution(mesh):
    placed = (P("pair", "col"), P("pair", "col"), P(), P("pair"))
    return jax.shard_map(
        per_device, mesh=mesh, in_specs=placed, out_specs=P("pair", "col"), check_vma=False
    )
```

```python
import functools

import jax
import jax.numpy as jnp
from jax import lax
from jax.experimental import pallas as pl
from jax.experimental.pallas import tpu as pltpu
from jax.sharding import PartitionSpec as P

MESH = pl.DeviceIdType.MESH
NX, NZ = 4, 8
TILE = 256
F32 = jnp.float32


def iota(shape, axis):
    return lax.broadcasted_iota(jnp.int32, shape, axis)


def kernel(
    cap, slots,
    start_ref, irr_ref, amp_ref, int_ref,
    out_ref, flag_ref,
    irr_all, comp, gat_a, gat_b, ints, pick, lhs, own, mix, low, acc, sendb, recvb,
    irr_send, irr_recv, a_send, a_recv, b_send, b_recv, z_send, z_recv, x_send, x_recv,
    int_send, int_recv, own_sem, ex_send, ex_recv, ready,
):
    pairs = irr_ref.shape[0]
    depth, cols = int_ref.shape
    rows = amp_ref.shape[0]
    part = rows // 2
    half = 2 * depth
    tiles = cols // TILE

    pair = lax.axis_index("pair")
    col = lax.axis_index("col")
    h, core = pair // 2, pair % 2
    yh, x, z = col // (NX * NZ), (col // NZ) % NX, col % NZ
    kind = (h == yh).astype(jnp.int32)
    selfish = h == yh

    def at(hh, cc, yy, xx, zz):
        return (hh * 2 + cc, (yy * NX + xx) * NZ + zz)

    def xs(d):
        return (x + NX + d) % NX

    def zs(d):
        return (z + NZ + d) % NZ

    def remote(src, dst, send, recv, dev):
        return pltpu.make_async_remote_copy(
            src_ref=src, dst_ref=dst, send_sem=send, recv_sem=recv, device_id=dev, device_id_type=MESH
        )

    sibling = at(h, 1 - core, yh, x, z)
    partner = at(1 - h, core, yh, x, z)

    barrier = pltpu.get_barrier_semaphore()

    def signal(dev):
        pl.semaphore_signal(barrier, inc=1, device_id=dev, device_id_type=MESH)

    near = [at(h, core, yh, x, zs(d)) for d in (1, -1, 2, -2)] + [at(h, core, yh, xs(d), z) for d in (1, -1)]

    @pl.when(core == 0)
    def _():
        signal(sibling)

    signal(partner)
    for dev in near:
        signal(dev)
    for u in range(2):
        for d in range(NX):
            if d:
                signal(at(u, core, h, xs(d), z))
        for d in range(NZ):
            if d:
                signal(at(u, core, h, x, zs(d)))

        @pl.when(jnp.logical_not(jnp.logical_and(selfish, u == h)))
        def _(u=u):
            pl.semaphore_signal(barrier, inc=2, device_id=at(u, core, h, x, z), device_id_type=MESH)

    own_copy = pltpu.make_async_copy(int_ref, ints.at[pl.ds(core * depth, depth)], own_sem)
    own_copy.start()

    def row_irrep(row):
        total = jnp.int32(0)
        for j in range(1, 8):
            total = total + (row >= start_ref[j]).astype(jnp.int32)
        return total

    eye = iota((pairs, pairs), 0) == iota((pairs, pairs), 1)
    below = iota((pairs, pairs), 1) < iota((pairs, pairs), 0)
    above = iota((pairs, pairs), 0) < iota((pairs, pairs), 1)

    def down(v):
        return jnp.sum(jnp.where(eye, v, 0.0), axis=1, keepdims=True)

    def touch(v, which):
        total = jnp.zeros_like(v)
        for r in range(8):
            meets = jnp.logical_and(start_ref[r] < half * (which + 1), start_ref[r + 1] > half * which)
            total = total + jnp.where(v == float(r), jnp.where(meets, 1.0, 0.0), 0.0)
        return total

    mine = irr_ref[...].reshape(1, pairs)
    irr_all[pair] = mine
    mine_l = mine.astype(F32)
    mine_s = down(mine_l)
    rank_s = jnp.sum(jnp.where(jnp.logical_and(below, mine_s == mine_l), 1.0, 0.0), axis=1, keepdims=True)
    here = row_irrep(col * rows).astype(F32)
    where_s = jnp.where(mine_s == here, rank_s, -1.0)
    chosen = jnp.where(where_s == iota((pairs, cap), 1).astype(F32), 1.0, 0.0).astype(jnp.bfloat16)
    block = jnp.dot(amp_ref[...], chosen, preferred_element_type=F32).astype(jnp.bfloat16)
    comp[...] = block

    @pl.when(selfish)
    def _():
        gat_a[1, z, x] = block[:part]
        gat_b[1, x, z] = block[part:]

    pick_own = (mine_s * 512.0 + rank_s).astype(jnp.int32) - iota((pairs, cap), 1)

    pl.semaphore_wait(barrier, 1 + len(near) + 2 * (NX + NZ - kind) + core)

    def a_copy(u, d):
        return remote(
            comp.at[pl.ds(0, part)], gat_a.at[kind, z, x], a_send.at[u * NX + d], a_recv.at[kind, x],
            at(yh, core, u, xs(d), z),
        )

    def b_copy(u, d):
        return remote(
            comp.at[pl.ds(part, part)], gat_b.at[kind, x, z], b_send.at[u * NZ + d], b_recv.at[kind, z],
            at(yh, core, u, x, zs(d)),
        )

    def first_hops(act):
        for d in (4, 3, 5, 2, 6, 1, 7):
            for u in range(2):
                act(b_copy(u, d))
                if d < NX:
                    act(a_copy(u, d))
        for u in range(2):
            @pl.when(jnp.logical_not(jnp.logical_and(selfish, u == yh)))
            def _(u=u):
                act(a_copy(u, 0))
                act(b_copy(u, 0))

    def irr_copy(k):
        g = pair if k < 2 else (1 - h) * 2 + core
        return remote(irr_all.at[g], irr_all.at[g], irr_send.at[k], irr_recv.at[k], partner if k == 0 else sibling)

    def irr_arrival(k):
        g = ((1 - h) * 2 + core, h * 2 + 1 - core, (1 - h) * 2 + 1 - core)[k]
        return remote(irr_all.at[g], irr_all.at[g], irr_send.at[k], irr_recv.at[k], sibling)

    int_copy = remote(int_ref, ints.at[pl.ds(core * depth, depth)], int_send, int_recv, sibling)
    int_arrival = remote(int_ref, ints.at[pl.ds((1 - core) * depth, depth)], int_send, int_recv, sibling)

    irr_copy(0).start()
    first_hops(lambda c: c.start())

    @pl.when(core == 1)
    def _():
        pl.semaphore_signal(ready, inc=1, device_id=sibling, device_id_type=MESH)
        int_copy.start()

    src_l = touch(mine_l, 1 - h)
    both_l = src_l * touch(mine_l, h)
    src_s, both_s = down(src_l), down(both_l)
    pos1 = jnp.sum(jnp.where(below, src_l, 0.0), axis=1, keepdims=True)
    pos2 = jnp.sum(src_l, axis=1, keepdims=True) + jnp.sum(jnp.where(below, both_l, 0.0), axis=1, keepdims=True)
    pos1 = jnp.where(src_s > 0.0, pos1, -1.0)
    pos2 = jnp.where(both_s > 0.0, pos2, -1.0)
    slot = iota((pairs, slots), 1).astype(F32)
    mix[...] = jnp.where(jnp.logical_or(pos1 == slot, pos2 == slot), 1.0, 0.0).astype(jnp.bfloat16)

    irr_arrival(0).wait_recv()
    theirs_l = irr_all[(1 - h) * 2 + core].astype(F32)
    theirs_s = down(theirs_l)
    rank_l = jnp.sum(jnp.where(jnp.logical_and(above, theirs_s == theirs_l), 1.0, 0.0), axis=0, keepdims=True)
    key_l = theirs_l * 512.0 + rank_l + 1.0
    src_l = touch(theirs_l, h)
    both_l = src_l * touch(theirs_l, 1 - h)
    src_s, both_s = down(src_l), down(both_l)
    pos1 = jnp.sum(jnp.where(above, src_s, 0.0), axis=0, keepdims=True)
    pos2 = jnp.sum(src_l, axis=1, keepdims=True) + jnp.sum(jnp.where(above, both_s, 0.0), axis=0, keepdims=True)
    pos1 = jnp.where(src_l > 0.0, pos1, -1.0)
    pos2 = jnp.where(both_l > 0.0, pos2, -1.0)
    slot = iota((slots, pairs), 0).astype(F32)
    is_low = pos2 == slot
    key_slot = jnp.sum(jnp.where(jnp.logical_or(pos1 == slot, is_low), key_l, 0.0), axis=1, keepdims=True)
    low[...] = jnp.sum(jnp.where(is_low, 1.0, 0.0), axis=1, keepdims=True)
    pick[...] = (key_slot - 1.0).astype(jnp.int32) - iota((slots, cap), 1)

    def z_ref(t, d, piece):
        ref = gat_a.at[t, zs(d)]
        return ref if piece is None else ref.at[pl.ds(piece * (NX // 2), NX // 2)]

    z_plan = (
        (0, 2, None), (0, -2, None), (0, 1, None), (0, -1, None),
        (-2, 1, None), (2, -1, None), (-2, 2, 0), (2, -2, 1),
    )

    def z_copy(t, i):
        d, to, piece = z_plan[i]
        ref = z_ref(t, d, piece)
        return remote(ref, ref, z_send.at[t, i], z_recv.at[t, i], at(h, core, yh, x, zs(to)))

    def z_arrival(t, i):
        d, to, piece = z_plan[i]
        ref = z_ref(t, d - to, piece)
        return remote(ref, ref, z_send.at[t, i], z_recv.at[t, i], at(h, core, yh, x, zs(to)))

    def x_ref(t, d, piece):
        ref = gat_b.at[t, xs(d)]
        return ref if piece is None else ref.at[pl.ds(piece * (NZ // 2), NZ // 2)]

    x_plan = ((0, 1, None), (0, -1, None), (-1, 1, 0), (1, -1, 1))

    def x_copy(t, i):
        d, to, piece = x_plan[i]
        ref = x_ref(t, d, piece)
        return remote(ref, ref, x_send.at[t, i], x_recv.at[t, i], at(h, core, yh, xs(to), z))

    def x_arrival(t, i):
        d, to, piece = x_plan[i]
        ref = x_ref(t, d - to, piece)
        return remote(ref, ref, x_send.at[t, i], x_recv.at[t, i], at(h, core, yh, xs(to), z))

    def unless_own(t, d, act):
        if t == 1 and d == 0:
            @pl.when(jnp.logical_not(selfish))
            def _():
                act()
        else:
            act()

    def gather_start(t):
        for d in range(NX):
            arrival = remote(comp.at[pl.ds(0, part)], gat_a.at[t, z, xs(d)], a_send.at[0], a_recv.at[t, xs(d)], partner)
            unless_own(t, d, arrival.wait_recv)
        for i in range(4):
            z_copy(t, i).start()
        for d in range(NZ):
            arrival = remote(comp.at[pl.ds(part, part)], gat_b.at[t, x, zs(d)], b_send.at[0], b_recv.at[t, zs(d)], partner)
            unless_own(t, d, arrival.wait_recv)
        for i in range(2):
            x_copy(t, i).start()

    def gather_rest(t):
        z_arrival(t, 0).wait_recv()
        z_copy(t, 4).start()
        z_copy(t, 6).start()
        z_arrival(t, 1).wait_recv()
        z_copy(t, 5).start()
        z_copy(t, 7).start()
        for i in range(2):
            x_arrival(t, i).wait_recv()
            x_copy(t, 2 + i).start()
        for i in range(2, 8):
            z_arrival(t, i).wait_recv()
        for i in range(2, 4):
            x_arrival(t, i).wait_recv()

    gather_start(0)

    @pl.when(core == 0)
    def _():
        pl.semaphore_wait(ready, 1)
        int_copy.start()

    irr_copy(1).start()
    irr_copy(2).start()

    gather_rest(0)

    def expand(t, keys, dst):
        for b in range(half // 128):
            here = row_irrep(h * half + b * 128) * 512
            one_hot = jnp.where(keys == here, 1.0, 0.0).astype(jnp.bfloat16)
            zz, xx = 2 * (b % (NZ // 2)), b // (NZ // 2)
            packed = jnp.concatenate(
                [gat_a[t, zz, xx], gat_b[t, xx, zz], gat_a[t, zz + 1, xx], gat_b[t, xx, zz + 1]], axis=0
            )
            full = lax.dot_general(one_hot, packed, (((1,), (1,)), ((), ())), preferred_element_type=F32)
            dst[:, pl.ds(b * 128, 128)] = full.astype(jnp.bfloat16)

    expand(0, pick[...], lhs)
    own_copy.wait()
    int_arrival.wait_recv()

    def ex_copy(j):
        return remote(sendb.at[j], recvb.at[j], ex_send.at[j], ex_recv.at[j], partner)

    @pl.loop(0, tiles + 1)
    def _(j):
        @pl.when(j < tiles)
        def _():
            full = jnp.dot(lhs[...], ints[:, pl.ds(pl.multiple_of(j * TILE, TILE), TILE)], preferred_element_type=F32)
            high = full.astype(jnp.bfloat16).astype(F32)
            sendb[j] = jnp.where(low[...] > 0.0, full - high, full).astype(jnp.bfloat16)

        @pl.when(j > 0)
        def _():
            ex_copy(j - 1).start()

    gather_start(1)
    irr_arrival(1).wait_recv()
    irr_arrival(2).wait_recv()
    fits = jnp.ones((1, 1), F32)
    for g in range(4):
        v = irr_all[g].astype(F32)
        for r in range(8):
            count = jnp.sum(jnp.where(v == float(r), 1.0, 0.0), axis=1, keepdims=True)
            fits = jnp.where(count > float(cap), 0.0, fits)
        src = touch(v, 1 - g // 2)
        need = jnp.sum(src + src * touch(v, g // 2), axis=1, keepdims=True)
        fits = jnp.where(need > float(slots), 0.0, fits)
    flag_ref[0] = jnp.sum(fits).astype(jnp.int32)

    gather_rest(1)
    expand(1, pick_own, own)

    @pl.loop(0, tiles)
    def _(j):
        acc[j] = jnp.dot(own[...], ints[:, pl.ds(pl.multiple_of(j * TILE, TILE), TILE)], preferred_element_type=F32)

    @pl.loop(0, tiles)
    def _(j):
        ex_copy(j).wait_recv()
        total = acc[j] + jnp.dot(mix[...], recvb[j], preferred_element_type=F32)
        out_ref[:, pl.ds(pl.multiple_of(j * TILE, TILE), TILE)] = total.astype(jnp.bfloat16)

    first_hops(lambda c: c.wait_send())
    for k in range(3):
        irr_copy(k).wait_send()
    int_copy.wait_send()
    for t in range(2):
        for i in range(8):
            z_copy(t, i).wait_send()
        for i in range(4):
            x_copy(t, i).wait_send()

    @pl.loop(0, tiles)
    def _(j):
        ex_copy(j).wait_send()


def ladder(cap, slots, collective_id, starts, irreps, amp, integrals):
    rows, pairs = amp.shape
    depth, cols = integrals.shape
    half, tiles = 2 * depth, cols // TILE
    bf16 = jnp.bfloat16
    dma = pltpu.SemaphoreType.DMA
    vmem = pl.BlockSpec(memory_space=pltpu.VMEM)
    return pl.pallas_call(
        functools.partial(kernel, cap, slots),
        out_shape=(jax.ShapeDtypeStruct((pairs, cols), bf16), jax.ShapeDtypeStruct((1,), jnp.int32)),
        in_specs=[pl.BlockSpec(memory_space=pltpu.SMEM), vmem, vmem, pl.BlockSpec(memory_space=pl.ANY)],
        out_specs=(vmem, pl.BlockSpec(memory_space=pltpu.SMEM)),
        scratch_shapes=[
            pltpu.VMEM((4, 1, pairs), jnp.int32),
            pltpu.VMEM((rows, cap), bf16),
            pltpu.VMEM((2, NZ, NX, rows // 2, cap), bf16),
            pltpu.VMEM((2, NX, NZ, rows // 2, cap), bf16),
            pltpu.VMEM((half, cols), bf16),
            pltpu.VMEM((slots, cap), jnp.int32),
            pltpu.VMEM((slots, half), bf16),
            pltpu.VMEM((pairs, half), bf16),
            pltpu.VMEM((pairs, slots), bf16),
            pltpu.VMEM((slots, 1), F32),
            pltpu.VMEM((tiles, pairs, TILE), F32),
            pltpu.VMEM((tiles, slots, TILE), bf16),
            pltpu.VMEM((tiles, slots, TILE), bf16),
            dma((3,)), dma((3,)), dma((2 * NX,)), dma((2, NX)), dma((2 * NZ,)), dma((2, NZ)),
            dma((2, 8)), dma((2, 8)), dma((2, 4)), dma((2, 4)),
            dma, dma, dma, dma((tiles,)), dma((tiles,)), pltpu.SemaphoreType.REGULAR,
        ],
        compiler_params=pltpu.CompilerParams(
            collective_id=collective_id, has_side_effects=True, vmem_limit_bytes=56 * 1024 * 1024
        ),
        name="ladder_" + str(slots),
    )(starts, irreps, amp, integrals)


def per_device(amplitudes, integrals, irrep_start, pair_irrep):
    pairs = amplitudes.shape[0]
    operands = (irrep_start, pair_irrep, amplitudes.T, integrals)
    out, fits = ladder(128, 448, 0, *operands)
    return lax.cond(
        fits[0] > 0,
        lambda *_: out,
        lambda *args: ladder(pairs, 2 * pairs, 1, *args)[0],
        *operands,
    )


def solution(mesh):
    placed = (P("pair", "col"), P("pair", "col"), P(), P("pair"))
    return jax.shard_map(
        per_device, mesh=mesh, in_specs=placed, out_specs=P("pair", "col"), check_vma=False
    )
```

```python
import functools

import jax
import jax.numpy as jnp
from jax import lax
from jax.experimental import pallas as pl
from jax.experimental.pallas import tpu as pltpu
from jax.sharding import PartitionSpec as P

MESH = pl.DeviceIdType.MESH
NX, NZ = 4, 8
TILE = 256
F32 = jnp.float32


def iota(shape, axis):
    return lax.broadcasted_iota(jnp.int32, shape, axis)


PART = 16
SIZES = (256, 304, 352, 448)
CAP = 128


class Place:
    def __init__(self):
        pair, col = lax.axis_index("pair"), lax.axis_index("col")
        self.pair, self.col = pair, col
        self.h, self.core = pair // 2, pair % 2
        self.yh, self.x, self.z = col // (NX * NZ), (col // NZ) % NX, col % NZ
        self.group = (1 - self.h) * 2 + self.core
        self.partner = self.at(1 - self.h, self.core, self.yh, self.x, self.z)
        self.sibling = self.at(self.h, 1 - self.core, self.yh, self.x, self.z)
        self.near = [self.along_z(d) for d in (1, -1, 2, -2)] + [self.along_x(d) for d in (1, -1)]

    def at(self, h, core, yh, x, z):
        return (h * 2 + core, (yh * NX + x) * NZ + z)

    def xs(self, d):
        return (self.x + NX + d) % NX

    def zs(self, d):
        return (self.z + NZ + d) % NZ

    def along_z(self, d):
        return self.at(self.h, self.core, self.yh, self.x, self.zs(d))

    def along_x(self, d):
        return self.at(self.h, self.core, self.yh, self.xs(d), self.z)


def remote(src, dst, send, recv, dev):
    return pltpu.make_async_remote_copy(
        src_ref=src, dst_ref=dst, send_sem=send, recv_sem=recv, device_id=dev, device_id_type=MESH
    )


def row_irrep(start_ref, row):
    total = jnp.int32(0)
    for j in range(1, 8):
        total = total + (row >= start_ref[j]).astype(jnp.int32)
    return total


def touch(start_ref, v, which, half):
    total = jnp.zeros_like(v)
    for r in range(8):
        meets = jnp.logical_and(start_ref[r] < half * (which + 1), start_ref[r + 1] > half * which)
        total = total + jnp.where(v == float(r), jnp.where(meets, 1.0, 0.0), 0.0)
    return total


def down(v):
    n = v.shape[1]
    return jnp.sum(jnp.where(iota((n, n), 0) == iota((n, n), 1), v, 0.0), axis=1, keepdims=True)


def expand(start_ref, first_row, half, keys, slab, column, dst):
    for b in range(half // 128):
        here = row_irrep(start_ref, first_row + b * 128) * 512
        one_hot = jnp.where(keys == here, 1.0, 0.0).astype(jnp.bfloat16)
        zz, xx = 2 * (b % (NZ // 2)), b // (NZ // 2)
        packed = jnp.concatenate([slab(zz, xx), column(xx, zz), slab(zz + 1, xx), column(xx, zz + 1)], axis=0)
        full = lax.dot_general(one_hot, packed, (((1,), (1,)), ((), ())), preferred_element_type=F32)
        dst[:, pl.ds(b * 128, 128)] = full.astype(jnp.bfloat16)


Z_PLAN = (
    (0, 2, None), (0, -2, None), (0, 1, None), (0, -1, None),
    (-2, 1, None), (2, -1, None), (-2, 2, 0), (2, -2, 1),
)
X_PLAN = ((0, 1, None), (0, -1, None), (-1, 1, 0), (1, -1, 1))


def hop(place, axis, i, src, dst, send, recv, arriving=False):
    d, to, piece = (Z_PLAN if axis == "z" else X_PLAN)[i]
    index = place.zs if axis == "z" else place.xs
    n = (NX if axis == "z" else NZ) // 2

    def view(ref):
        ref = ref.at[index(d - to if arriving else d)]
        return ref if piece is None else ref.at[pl.ds(piece * n, n)]

    return remote(view(src), view(dst), send, recv, place.along_z(to) if axis == "z" else place.along_x(to))


def first_kernel(
    cap, slots,
    start_ref, irr_ref, amp_ref, int_ref,
    lhs, low, ints, gat_a, gat_b, irr_all, size_ref,
    comp,
    irr_send, irr_recv, a_send, a_recv, b_send, b_recv, z_send, z_recv, x_send, x_recv,
    int_send, int_recv, own_sem, ready,
):
    p = Place()
    pairs = irr_ref.shape[0]
    depth, cols = int_ref.shape
    rows = amp_ref.shape[0]
    half = 2 * depth
    kind = (p.h == p.yh).astype(jnp.int32)
    selfish = p.h == p.yh

    barrier = pltpu.get_barrier_semaphore()

    def signal(dev, inc=1):
        pl.semaphore_signal(barrier, inc=inc, device_id=dev, device_id_type=MESH)

    @pl.when(p.core == 0)
    def _():
        signal(p.sibling)

    signal(p.partner)
    for dev in p.near:
        signal(dev)
    for u in range(2):
        for d in range(1, NX):
            signal(p.at(u, p.core, p.h, p.xs(d), p.z))
        for d in range(1, NZ):
            signal(p.at(u, p.core, p.h, p.x, p.zs(d)))

        @pl.when(jnp.logical_not(jnp.logical_and(selfish, u == p.h)))
        def _(u=u):
            signal(p.at(u, p.core, p.h, p.x, p.z), 2)

    own_copy = pltpu.make_async_copy(int_ref, ints.at[pl.ds(p.core * depth, depth)], own_sem)
    own_copy.start()

    mine = irr_ref[...].reshape(1, pairs)
    irr_all[p.pair] = mine
    mine_l = mine.astype(F32)
    mine_s = down(mine_l)
    below = iota((pairs, pairs), 1) < iota((pairs, pairs), 0)
    rank_s = jnp.sum(jnp.where(jnp.logical_and(below, mine_s == mine_l), 1.0, 0.0), axis=1, keepdims=True)
    here = row_irrep(start_ref, p.col * rows).astype(F32)
    where_s = jnp.where(mine_s == here, rank_s, -1.0)
    chosen = jnp.where(where_s == iota((pairs, cap), 1).astype(F32), 1.0, 0.0).astype(jnp.bfloat16)
    block = jnp.dot(amp_ref[...], chosen, preferred_element_type=F32).astype(jnp.bfloat16)
    comp[...] = block

    @pl.when(selfish)
    def _():
        gat_a[1, p.z, p.x] = block[:PART]
        gat_b[1, p.x, p.z] = block[PART:]

    pl.semaphore_wait(barrier, 1 + len(p.near) + 2 * (NX + NZ - kind) + p.core)

    comp_a, comp_b = comp.at[pl.ds(0, PART)], comp.at[pl.ds(PART, rows - PART)]

    def a_copy(u, d):
        dev = p.at(p.yh, p.core, u, p.xs(d), p.z)
        return remote(comp_a, gat_a.at[kind, p.z, p.x], a_send.at[u * NX + d], a_recv.at[kind, p.x], dev)

    def b_copy(u, d):
        dev = p.at(p.yh, p.core, u, p.x, p.zs(d))
        return remote(comp_b, gat_b.at[kind, p.x, p.z], b_send.at[u * NZ + d], b_recv.at[kind, p.z], dev)

    def first_hops(act):
        for d in (4, 3, 5, 2, 6, 1, 7):
            for u in range(2):
                act(b_copy(u, d))
                if d < NX:
                    act(a_copy(u, d))
        for u in range(2):
            @pl.when(jnp.logical_not(jnp.logical_and(selfish, u == p.yh)))
            def _(u=u):
                act(a_copy(u, 0))
                act(b_copy(u, 0))

    def irr_copy(k):
        g = p.pair if k < 2 else p.group
        dev = p.partner if k == 0 else p.sibling
        return remote(irr_all.at[g], irr_all.at[g], irr_send.at[k], irr_recv.at[k], dev)

    def irr_arrival(k):
        g = (p.group, p.h * 2 + 1 - p.core, (1 - p.h) * 2 + 1 - p.core)[k]
        return remote(irr_all.at[g], irr_all.at[g], irr_send.at[k], irr_recv.at[k], p.sibling)

    int_copy = remote(int_ref, ints.at[pl.ds(p.core * depth, depth)], int_send, int_recv, p.sibling)
    int_arrival = remote(int_ref, ints.at[pl.ds((1 - p.core) * depth, depth)], int_send, int_recv, p.sibling)

    irr_copy(0).start()
    first_hops(lambda c: c.start())

    @pl.when(p.core == 1)
    def _():
        pl.semaphore_signal(ready, inc=1, device_id=p.sibling, device_id_type=MESH)

    @pl.when(p.core == 0)
    def _():
        pl.semaphore_wait(ready, 1)

    int_copy.start()
    irr_copy(1).start()

    irr_arrival(0).wait_recv()
    irr_copy(2).start()
    theirs_l = irr_all[p.group].astype(F32)
    theirs_s = down(theirs_l)
    above = iota((pairs, pairs), 0) < iota((pairs, pairs), 1)
    rank_l = jnp.sum(jnp.where(jnp.logical_and(above, theirs_s == theirs_l), 1.0, 0.0), axis=0, keepdims=True)
    key_l = theirs_l * 512.0 + rank_l + 1.0
    src_l = touch(start_ref, theirs_l, p.h, half)
    both_l = src_l * touch(start_ref, theirs_l, 1 - p.h, half)
    src_s, both_s = down(src_l), down(both_l)
    pos1 = jnp.sum(jnp.where(above, src_s, 0.0), axis=0, keepdims=True)
    pos2 = jnp.sum(src_l, axis=1, keepdims=True) + jnp.sum(jnp.where(above, both_s, 0.0), axis=0, keepdims=True)
    pos1 = jnp.where(src_l > 0.0, pos1, -1.0)
    pos2 = jnp.where(both_l > 0.0, pos2, -1.0)
    slot = iota((slots, pairs), 0).astype(F32)
    is_low = pos2 == slot
    key_slot = jnp.sum(jnp.where(jnp.logical_or(pos1 == slot, is_low), key_l, 0.0), axis=1, keepdims=True)
    low[...] = jnp.sum(jnp.where(is_low, 1.0, 0.0), axis=1, keepdims=True)
    pick = (key_slot - 1.0).astype(jnp.int32) - iota((slots, cap), 1)

    def z_hop(t, i, arriving=False):
        return hop(p, "z", i, gat_a.at[t], gat_a.at[t], z_send.at[t, i], z_recv.at[t, i], arriving)

    def x_hop(t, i, arriving=False):
        return hop(p, "x", i, gat_b.at[t], gat_b.at[t], x_send.at[t, i], x_recv.at[t, i], arriving)

    def unless_own(t, d, act):
        if t == 1 and d == 0:
            @pl.when(jnp.logical_not(selfish))
            def _():
                act()
        else:
            act()

    def gather_start(t):
        for d in range(NZ):
            arrival = remote(comp_b, gat_b.at[t, p.x, p.zs(d)], b_send.at[0], b_recv.at[t, p.zs(d)], p.partner)
            unless_own(t, d, arrival.wait_recv)
        for i in range(2):
            x_hop(t, i).start()
        for d in range(NX):
            arrival = remote(comp_a, gat_a.at[t, p.z, p.xs(d)], a_send.at[0], a_recv.at[t, p.xs(d)], p.partner)
            unless_own(t, d, arrival.wait_recv)
        for i in range(4):
            z_hop(t, i).start()

    gather_start(0)
    for i in range(2):
        x_hop(0, i, True).wait_recv()
        x_hop(0, 2 + i).start()
    for i in range(2):
        z_hop(0, i, True).wait_recv()
        z_hop(0, 4 + i).start()
        z_hop(0, 6 + i).start()
    gather_start(1)

    irr_arrival(1).wait_recv()
    irr_arrival(2).wait_recv()
    most = jnp.zeros((1, 1), F32)
    for g in range(4):
        v = irr_all[g].astype(F32)
        for r in range(8):
            count = jnp.sum(jnp.where(v == float(r), 1.0, 0.0), axis=1, keepdims=True)
            most = jnp.where(count > float(cap), 1e6, most)
        src = touch(start_ref, v, 1 - g // 2, half)
        need = jnp.sum(src + src * touch(start_ref, v, g // 2, half), axis=1, keepdims=True)
        most = jnp.maximum(most, need)
    choice = jnp.zeros((1, 1), F32)
    for size in SIZES:
        choice = choice + jnp.where(most <= float(size), 1.0, 0.0)
    size_ref[0] = jnp.sum(choice).astype(jnp.int32)

    for i in range(2, 4):
        x_hop(0, i, True).wait_recv()
    for i in range(2, 8):
        z_hop(0, i, True).wait_recv()
    expand(
        start_ref, p.h * half, half, pick,
        lambda zz, xx: gat_a[0, zz, xx], lambda xx, zz: gat_b[0, xx, zz], lhs,
    )
    for i in range(2):
        x_hop(1, i, True).wait_recv()
    for i in range(4):
        z_hop(1, i, True).wait_recv()
    own_copy.wait()
    int_arrival.wait_recv()

    first_hops(lambda c: c.wait_send())
    for k in range(3):
        irr_copy(k).wait_send()
    int_copy.wait_send()
    for t in range(2):
        for i in range(4 if t else 8):
            z_hop(t, i).wait_send()
        for i in range(2 if t else 4):
            x_hop(t, i).wait_send()


def second_kernel(
    cap, slots,
    start_ref, lhs, low, ints, gat_a, gat_b, irr_all,
    out_ref,
    slabs, columns, own, mix, acc, sendb, recvb,
    z_send, z_recv, x_send, x_recv, ex_send, ex_recv,
):
    p = Place()
    pairs = irr_all.shape[2]
    half, cols = ints.shape
    tiles = cols // TILE

    barrier = pltpu.get_barrier_semaphore()
    for dev in p.near + [p.partner]:
        pl.semaphore_signal(barrier, inc=1, device_id=dev, device_id_type=MESH)

    def span(j):
        return pl.ds(pl.multiple_of(j * TILE, TILE), TILE)

    def product(j):
        full = jnp.dot(lhs[pl.ds(0, slots), :], ints[:, span(j)], preferred_element_type=F32)
        high = full.astype(jnp.bfloat16).astype(F32)
        sendb[j] = jnp.where(low[pl.ds(0, slots), :] > 0.0, full - high, full).astype(jnp.bfloat16)

    def ex_copy(j):
        return remote(sendb.at[j], recvb.at[j], ex_send.at[j], ex_recv.at[j], p.partner)

    product(0)
    pl.semaphore_wait(barrier, len(p.near) + 1)

    def z_hop(i, arriving=False):
        return hop(p, "z", i, gat_a.at[1], slabs, z_send.at[i - 4], z_recv.at[i - 4], arriving)

    def x_hop(i, arriving=False):
        return hop(p, "x", i, gat_b.at[1], columns, x_send.at[i - 2], x_recv.at[i - 2], arriving)

    for i in range(2, 4):
        x_hop(i).start()
    for i in range(4, 8):
        z_hop(i).start()

    @pl.loop(1, tiles)
    def _(j):
        product(j)
        ex_copy(j - 1).start()

    mine_l = irr_all[p.pair].astype(F32)
    mine_s = down(mine_l)
    below = iota((pairs, pairs), 1) < iota((pairs, pairs), 0)
    rank_s = jnp.sum(jnp.where(jnp.logical_and(below, mine_s == mine_l), 1.0, 0.0), axis=1, keepdims=True)
    ex_copy(tiles - 1).start()
    src_l = touch(start_ref, mine_l, 1 - p.h, half)
    both_l = src_l * touch(start_ref, mine_l, p.h, half)
    src_s, both_s = down(src_l), down(both_l)
    pos1 = jnp.sum(jnp.where(below, src_l, 0.0), axis=1, keepdims=True)
    pos2 = jnp.sum(src_l, axis=1, keepdims=True) + jnp.sum(jnp.where(below, both_l, 0.0), axis=1, keepdims=True)
    pos1 = jnp.where(src_s > 0.0, pos1, -1.0)
    pos2 = jnp.where(both_s > 0.0, pos2, -1.0)
    slot = iota((pairs, slots), 1).astype(F32)
    mix[...] = jnp.where(jnp.logical_or(pos1 == slot, pos2 == slot), 1.0, 0.0).astype(jnp.bfloat16)
    pick = (mine_s * 512.0 + rank_s).astype(jnp.int32) - iota((pairs, cap), 1)

    for d in range(-2, 3):
        slabs[p.zs(d)] = gat_a[1, p.zs(d)]
    for d in range(-1, 2):
        columns[p.xs(d)] = gat_b[1, p.xs(d)]
    for i in range(2, 4):
        x_hop(i, True).wait_recv()
    for i in range(4, 8):
        z_hop(i, True).wait_recv()
    expand(start_ref, p.h * half, half, pick, lambda zz, xx: slabs[zz, xx], lambda xx, zz: columns[xx, zz], own)

    @pl.loop(0, tiles)
    def _(j):
        acc[j] = jnp.dot(own[...], ints[:, span(j)], preferred_element_type=F32)

    @pl.loop(0, tiles)
    def _(j):
        ex_copy(j).wait_recv()
        total = acc[j] + jnp.dot(mix[...], recvb[j], preferred_element_type=F32)
        out_ref[:, span(j)] = total.astype(jnp.bfloat16)

    for i in range(2, 4):
        x_hop(i).wait_send()
    for i in range(4, 8):
        z_hop(i).wait_send()

    @pl.loop(0, tiles)
    def _(j):
        ex_copy(j).wait_send()


DMA = pltpu.SemaphoreType.DMA
VMEM_SPEC = pl.BlockSpec(memory_space=pltpu.VMEM)
SMEM_SPEC = pl.BlockSpec(memory_space=pltpu.SMEM)


def params(collective_id):
    return pltpu.CompilerParams(
        collective_id=collective_id, has_side_effects=True, vmem_limit_bytes=32 * 1024 * 1024
    )


def first(cap, slots, collective_id, starts, irreps, amp, integrals):
    rows, pairs = amp.shape
    depth, cols = integrals.shape
    bf16 = jnp.bfloat16
    shape = jax.ShapeDtypeStruct
    return pl.pallas_call(
        functools.partial(first_kernel, cap, slots),
        out_shape=(
            shape((slots, 2 * depth), bf16), shape((slots, 1), F32), shape((2 * depth, cols), bf16),
            shape((2, NZ, NX, PART, cap), bf16), shape((2, NX, NZ, rows - PART, cap), bf16),
            shape((4, 1, pairs), jnp.int32), shape((1,), jnp.int32),
        ),
        in_specs=[SMEM_SPEC, VMEM_SPEC, VMEM_SPEC, pl.BlockSpec(memory_space=pl.ANY)],
        out_specs=(VMEM_SPEC,) * 6 + (SMEM_SPEC,),
        scratch_shapes=[
            pltpu.VMEM((rows, cap), bf16),
            DMA((3,)), DMA((3,)), DMA((2 * NX,)), DMA((2, NX)), DMA((2 * NZ,)), DMA((2, NZ)),
            DMA((2, 8)), DMA((2, 8)), DMA((2, 4)), DMA((2, 4)),
            DMA, DMA, DMA, pltpu.SemaphoreType.REGULAR,
        ],
        compiler_params=params(collective_id),
        name="gather_" + str(slots),
    )(starts, irreps, amp, integrals)


def second(cap, slots, collective_id, starts, lhs, low, ints, gat_a, gat_b, irr_all):
    pairs, cols, half = irr_all.shape[2], ints.shape[1], ints.shape[0]
    tiles = cols // TILE
    bf16 = jnp.bfloat16
    return pl.pallas_call(
        functools.partial(second_kernel, cap, slots),
        out_shape=jax.ShapeDtypeStruct((pairs, cols), bf16),
        in_specs=[SMEM_SPEC] + [VMEM_SPEC] * 6,
        out_specs=VMEM_SPEC,
        scratch_shapes=[
            pltpu.VMEM(gat_a.shape[1:], bf16),
            pltpu.VMEM(gat_b.shape[1:], bf16),
            pltpu.VMEM((pairs, half), bf16),
            pltpu.VMEM((pairs, slots), bf16),
            pltpu.VMEM((tiles, pairs, TILE), F32),
            pltpu.VMEM((tiles, slots, TILE), bf16),
            pltpu.VMEM((tiles, slots, TILE), bf16),
            DMA((4,)), DMA((4,)), DMA((2,)), DMA((2,)), DMA((tiles,)), DMA((tiles,)),
        ],
        compiler_params=params(collective_id),
        name="exchange_" + str(slots),
    )(starts, lhs, low, ints, gat_a, gat_b, irr_all)


def per_device(amplitudes, integrals, irrep_start, pair_irrep):
    pairs = amplitudes.shape[0]
    operands = (irrep_start, pair_irrep, amplitudes.T, integrals)
    *state, size = first(CAP, SIZES[-1], 0, *operands)

    def full(state, operands):
        *state, _ = first(pairs, 2 * pairs, 1, *operands)
        return second(pairs, 2 * pairs, 2, operands[0], *state)

    def sized(slots, collective_id):
        return lambda state, operands: second(CAP, slots, collective_id, operands[0], *state)

    branches = [full] + [sized(slots, 3 + i) for i, slots in enumerate(reversed(SIZES))]
    return lax.switch(size[0], branches, state, operands)


def solution(mesh):
    placed = (P("pair", "col"), P("pair", "col"), P(), P("pair"))
    return jax.shard_map(
        per_device, mesh=mesh, in_specs=placed, out_specs=P("pair", "col"), check_vma=False
    )
```

```python
import functools

import jax
import jax.numpy as jnp
from jax import lax
from jax.experimental import pallas as pl
from jax.experimental.pallas import tpu as pltpu
from jax.sharding import PartitionSpec as P

MESH = pl.DeviceIdType.MESH
NX, NZ = 4, 8
TILE = 256
F32 = jnp.float32


def iota(shape, axis):
    return lax.broadcasted_iota(jnp.int32, shape, axis)


PART = 16
SIZES = (256, 304, 352, 416, 448)
CAP = 128


class Place:
    def __init__(self):
        pair, col = lax.axis_index("pair"), lax.axis_index("col")
        self.pair, self.col = pair, col
        self.h, self.core = pair // 2, pair % 2
        self.yh, self.x, self.z = col // (NX * NZ), (col // NZ) % NX, col % NZ
        self.group = (1 - self.h) * 2 + self.core
        self.partner = self.at(1 - self.h, self.core, self.yh, self.x, self.z)
        self.sibling = self.at(self.h, 1 - self.core, self.yh, self.x, self.z)
        self.near = [self.along_x(d) for d in (1, -1)]

    def at(self, h, core, yh, x, z):
        return (h * 2 + core, (yh * NX + x) * NZ + z)

    def xs(self, d):
        return (self.x + NX + d) % NX

    def zs(self, d):
        return (self.z + NZ + d) % NZ

    def along_z(self, d):
        return self.at(self.h, self.core, self.yh, self.x, self.zs(d))

    def along_x(self, d):
        return self.at(self.h, self.core, self.yh, self.xs(d), self.z)


def remote(src, dst, send, recv, dev):
    return pltpu.make_async_remote_copy(
        src_ref=src, dst_ref=dst, send_sem=send, recv_sem=recv, device_id=dev, device_id_type=MESH
    )


def row_irrep(start_ref, row):
    total = jnp.int32(0)
    for j in range(1, 8):
        total = total + (row >= start_ref[j]).astype(jnp.int32)
    return total


def touch(start_ref, v, which, half):
    total = jnp.zeros_like(v)
    for r in range(8):
        meets = jnp.logical_and(start_ref[r] < half * (which + 1), start_ref[r + 1] > half * which)
        total = total + jnp.where(v == float(r), jnp.where(meets, 1.0, 0.0), 0.0)
    return total


def down(v):
    n = v.shape[1]
    return jnp.sum(jnp.where(iota((n, n), 0) == iota((n, n), 1), v, 0.0), axis=1, keepdims=True)


def expand(start_ref, first_row, half, keys, slab, column, dst):
    for b in range(half // 128):
        here = row_irrep(start_ref, first_row + b * 128) * 512
        one_hot = jnp.where(keys == here, 1.0, 0.0).astype(jnp.bfloat16)
        zz, xx = 2 * (b % (NZ // 2)), b // (NZ // 2)
        packed = jnp.concatenate([slab(zz, xx), column(xx, zz), slab(zz + 1, xx), column(xx, zz + 1)], axis=0)
        full = lax.dot_general(one_hot, packed, (((1,), (1,)), ((), ())), preferred_element_type=F32)
        dst[:, pl.ds(b * 128, 128)] = full.astype(jnp.bfloat16)


Z_PLAN = tuple((0, d, None) for d in (4, 3, -3, 2, -2, 1, -1))
X_PLAN = ((0, 1, 0), (0, -1, 1), (0, 1, 1), (0, -1, 0), (-1, 1, 0), (1, -1, 1))
X_NEAR = 4


def hop(place, axis, i, src, dst, send, recv, arriving=False):
    d, to, piece = (Z_PLAN if axis == "z" else X_PLAN)[i]
    index = place.zs if axis == "z" else place.xs
    n = (NX if axis == "z" else NZ) // 2

    def view(ref):
        ref = ref.at[index(d - to if arriving else d)]
        return ref if piece is None else ref.at[pl.ds(piece * n, n)]

    return remote(view(src), view(dst), send, recv, place.along_z(to) if axis == "z" else place.along_x(to))


def first_kernel(
    cap, slots,
    start_hbm, irr_hbm, amp_hbm, int_ref,
    lhs, low, ints, gat_a, gat_b, irr_all, size_ref,
    comp, start_ref, irr_ref, amp_ref, load_sem,
    irr_send, irr_recv, a_send, a_recv, b_send, b_recv, z_send, z_recv, x_send, x_recv,
    int_send, int_recv, own_sem, ready,
):
    p = Place()
    pairs = irr_ref.shape[0]
    depth, cols = int_ref.shape
    rows = amp_ref.shape[0]
    half = 2 * depth
    kind = (p.h == p.yh).astype(jnp.int32)
    selfish = p.h == p.yh

    loads = [
        pltpu.make_async_copy(src, dst, load_sem.at[i])
        for i, (src, dst) in enumerate(((irr_hbm, irr_ref), (start_hbm, start_ref), (amp_hbm, amp_ref)))
    ]
    for load in loads:
        load.start()

    barrier = pltpu.get_barrier_semaphore()

    def signal(dev, inc=1):
        pl.semaphore_signal(barrier, inc=inc, device_id=dev, device_id_type=MESH)

    @pl.when(p.core == 0)
    def _():
        signal(p.sibling)

    signal(p.partner)
    for dev in p.near + [p.along_z(d) for _, d, _ in Z_PLAN]:
        signal(dev)
    for u in range(2):
        for d in range(1, NX):
            signal(p.at(u, p.core, p.h, p.xs(d), p.z))
        for d in range(1, NZ):
            signal(p.at(u, p.core, p.h, p.x, p.zs(d)))

        @pl.when(jnp.logical_not(jnp.logical_and(selfish, u == p.h)))
        def _(u=u):
            signal(p.at(u, p.core, p.h, p.x, p.z), 2)

    own_copy = pltpu.make_async_copy(int_ref, ints.at[pl.ds(p.core * depth, depth)], own_sem)
    own_copy.start()
    for load in loads:
        load.wait()

    mine = irr_ref[...].reshape(1, pairs)
    irr_all[p.pair] = mine
    mine_l = mine.astype(F32)
    mine_s = down(mine_l)
    below = iota((pairs, pairs), 1) < iota((pairs, pairs), 0)
    rank_s = jnp.sum(jnp.where(jnp.logical_and(below, mine_s == mine_l), 1.0, 0.0), axis=1, keepdims=True)
    here = row_irrep(start_ref, p.col * rows).astype(F32)
    where_s = jnp.where(mine_s == here, rank_s, -1.0)
    chosen = jnp.where(where_s == iota((pairs, cap), 1).astype(F32), 1.0, 0.0).astype(jnp.bfloat16)
    block = jnp.dot(amp_ref[...], chosen, preferred_element_type=F32).astype(jnp.bfloat16)
    comp[...] = block

    @pl.when(selfish)
    def _():
        gat_a[1, p.z, p.x] = block[:PART]
        gat_b[1, p.x, p.z] = block[PART:]

    pl.semaphore_wait(barrier, 1 + len(p.near) + len(Z_PLAN) + 2 * (NX + NZ - kind) + p.core)

    comp_a, comp_b = comp.at[pl.ds(0, PART)], comp.at[pl.ds(PART, rows - PART)]

    def a_copy(u, d):
        dev = p.at(p.yh, p.core, u, p.xs(d), p.z)
        return remote(comp_a, gat_a.at[kind, p.z, p.x], a_send.at[u * NX + d], a_recv.at[kind, p.x], dev)

    def b_copy(u, d):
        dev = p.at(p.yh, p.core, u, p.x, p.zs(d))
        return remote(comp_b, gat_b.at[kind, p.x, p.z], b_send.at[u * NZ + d], b_recv.at[kind, p.z], dev)

    def first_hops(act):
        for d in (4, 3, 5, 2, 6, 1, 7):
            for u in range(2):
                act(b_copy(u, d))
                if d < NX:
                    act(a_copy(u, d))
        for u in range(2):
            @pl.when(jnp.logical_not(jnp.logical_and(selfish, u == p.yh)))
            def _(u=u):
                act(a_copy(u, 0))
                act(b_copy(u, 0))

    def irr_copy(k):
        g = p.pair if k < 2 else p.group
        dev = p.partner if k == 0 else p.sibling
        return remote(irr_all.at[g], irr_all.at[g], irr_send.at[k], irr_recv.at[k], dev)

    def irr_arrival(k):
        g = (p.group, p.h * 2 + 1 - p.core, (1 - p.h) * 2 + 1 - p.core)[k]
        return remote(irr_all.at[g], irr_all.at[g], irr_send.at[k], irr_recv.at[k], p.sibling)

    int_copy = remote(int_ref, ints.at[pl.ds(p.core * depth, depth)], int_send, int_recv, p.sibling)
    int_arrival = remote(int_ref, ints.at[pl.ds((1 - p.core) * depth, depth)], int_send, int_recv, p.sibling)

    irr_copy(0).start()
    first_hops(lambda c: c.start())

    @pl.when(p.core == 1)
    def _():
        pl.semaphore_signal(ready, inc=1, device_id=p.sibling, device_id_type=MESH)

    @pl.when(p.core == 0)
    def _():
        pl.semaphore_wait(ready, 1)

    int_copy.start()
    irr_copy(1).start()

    irr_arrival(0).wait_recv()
    irr_copy(2).start()
    theirs_l = irr_all[p.group].astype(F32)
    theirs_s = down(theirs_l)
    above = iota((pairs, pairs), 0) < iota((pairs, pairs), 1)
    rank_l = jnp.sum(jnp.where(jnp.logical_and(above, theirs_s == theirs_l), 1.0, 0.0), axis=0, keepdims=True)
    key_l = theirs_l * 512.0 + rank_l + 1.0
    src_l = touch(start_ref, theirs_l, p.h, half)
    both_l = src_l * touch(start_ref, theirs_l, 1 - p.h, half)
    src_s, both_s = down(src_l), down(both_l)
    pos1 = jnp.sum(jnp.where(above, src_s, 0.0), axis=0, keepdims=True)
    pos2 = jnp.sum(src_l, axis=1, keepdims=True) + jnp.sum(jnp.where(above, both_s, 0.0), axis=0, keepdims=True)
    pos1 = jnp.where(src_l > 0.0, pos1, -1.0)
    pos2 = jnp.where(both_l > 0.0, pos2, -1.0)
    slot = iota((slots, pairs), 0).astype(F32)
    is_low = pos2 == slot
    key_slot = jnp.sum(jnp.where(jnp.logical_or(pos1 == slot, is_low), key_l, 0.0), axis=1, keepdims=True)
    low[...] = jnp.sum(jnp.where(is_low, 1.0, 0.0), axis=1, keepdims=True)
    pick = (key_slot - 1.0).astype(jnp.int32) - iota((slots, cap), 1)

    def z_hop(t, i, arriving=False):
        return hop(p, "z", i, gat_a.at[t], gat_a.at[t], z_send.at[t, i], z_recv.at[t, i], arriving)

    def x_hop(t, i, arriving=False):
        return hop(p, "x", i, gat_b.at[t], gat_b.at[t], x_send.at[t, i], x_recv.at[t, i], arriving)

    def unless_own(t, d, act):
        if t == 1 and d == 0:
            @pl.when(jnp.logical_not(selfish))
            def _():
                act()
        else:
            act()

    def gather_start(t):
        for d in range(NZ):
            arrival = remote(comp_b, gat_b.at[t, p.x, p.zs(d)], b_send.at[0], b_recv.at[t, p.zs(d)], p.partner)
            unless_own(t, d, arrival.wait_recv)
        for i in range(X_NEAR):
            x_hop(t, i).start()
        for d in range(NX):
            arrival = remote(comp_a, gat_a.at[t, p.z, p.xs(d)], a_send.at[0], a_recv.at[t, p.xs(d)], p.partner)
            unless_own(t, d, arrival.wait_recv)
        for i in range(len(Z_PLAN)):
            z_hop(t, i).start()

    gather_start(0)
    for i in range(2):
        x_hop(0, i, True).wait_recv()
        x_hop(0, X_NEAR + i).start()
    gather_start(1)

    irr_arrival(1).wait_recv()
    irr_arrival(2).wait_recv()
    most = jnp.zeros((1, 1), F32)
    for g in range(4):
        v = irr_all[g].astype(F32)
        for r in range(8):
            count = jnp.sum(jnp.where(v == float(r), 1.0, 0.0), axis=1, keepdims=True)
            most = jnp.where(count > float(cap), 1e6, most)
        src = touch(start_ref, v, 1 - g // 2, half)
        need = jnp.sum(src + src * touch(start_ref, v, g // 2, half), axis=1, keepdims=True)
        most = jnp.maximum(most, need)
    choice = jnp.zeros((1, 1), F32)
    for size in SIZES:
        choice = choice + jnp.where(most <= float(size), 1.0, 0.0)
    size_ref[0] = jnp.sum(choice).astype(jnp.int32)

    for i in range(2, len(X_PLAN)):
        x_hop(0, i, True).wait_recv()
    for i in range(len(Z_PLAN)):
        z_hop(0, i, True).wait_recv()
    expand(
        start_ref, p.h * half, half, pick,
        lambda zz, xx: gat_a[0, zz, xx], lambda xx, zz: gat_b[0, xx, zz], lhs,
    )
    for i in range(X_NEAR):
        x_hop(1, i, True).wait_recv()
    for i in range(len(Z_PLAN)):
        z_hop(1, i, True).wait_recv()
    own_copy.wait()
    int_arrival.wait_recv()

    first_hops(lambda c: c.wait_send())
    for k in range(3):
        irr_copy(k).wait_send()
    int_copy.wait_send()
    for t in range(2):
        for i in range(len(Z_PLAN)):
            z_hop(t, i).wait_send()
        for i in range(X_NEAR if t else len(X_PLAN)):
            x_hop(t, i).wait_send()


def second_kernel(
    cap, slots,
    start_hbm, lhs, low, ints, gat_a, gat_b, irr_all,
    out_ref,
    start_ref, load_sem, columns, own, mix, acc, sendb, recvb,
    x_send, x_recv, ex_send, ex_recv,
):
    p = Place()
    pairs = irr_all.shape[2]
    half, cols = ints.shape
    tiles = cols // TILE

    barrier = pltpu.get_barrier_semaphore()
    for dev in p.near + [p.partner]:
        pl.semaphore_signal(barrier, inc=1, device_id=dev, device_id_type=MESH)
    load = pltpu.make_async_copy(start_hbm, start_ref, load_sem)
    load.start()

    def span(j):
        return pl.ds(pl.multiple_of(j * TILE, TILE), TILE)

    def product(j):
        full = jnp.dot(lhs[pl.ds(0, slots), :], ints[:, span(j)], preferred_element_type=F32)
        high = full.astype(jnp.bfloat16).astype(F32)
        sendb[j] = jnp.where(low[pl.ds(0, slots), :] > 0.0, full - high, full).astype(jnp.bfloat16)

    def ex_copy(j):
        return remote(sendb.at[j], recvb.at[j], ex_send.at[j], ex_recv.at[j], p.partner)

    product(0)
    pl.semaphore_wait(barrier, len(p.near) + 1)

    def x_hop(i, arriving=False):
        return hop(p, "x", i, gat_b.at[1], columns, x_send.at[i - X_NEAR], x_recv.at[i - X_NEAR], arriving)

    for i in range(X_NEAR, len(X_PLAN)):
        x_hop(i).start()

    load.wait()
    ex_copy(0).start()
    product(1)

    @pl.loop(2, tiles)
    def _(j):
        product(j)
        ex_copy(j - 1).start()

    mine_l = irr_all[p.pair].astype(F32)
    mine_s = down(mine_l)
    below = iota((pairs, pairs), 1) < iota((pairs, pairs), 0)
    rank_s = jnp.sum(jnp.where(jnp.logical_and(below, mine_s == mine_l), 1.0, 0.0), axis=1, keepdims=True)
    ex_copy(tiles - 1).start()
    src_l = touch(start_ref, mine_l, 1 - p.h, half)
    both_l = src_l * touch(start_ref, mine_l, p.h, half)
    src_s, both_s = down(src_l), down(both_l)
    pos1 = jnp.sum(jnp.where(below, src_l, 0.0), axis=1, keepdims=True)
    pos2 = jnp.sum(src_l, axis=1, keepdims=True) + jnp.sum(jnp.where(below, both_l, 0.0), axis=1, keepdims=True)
    pos1 = jnp.where(src_s > 0.0, pos1, -1.0)
    pos2 = jnp.where(both_s > 0.0, pos2, -1.0)
    slot = iota((pairs, slots), 1).astype(F32)
    mix[...] = jnp.where(jnp.logical_or(pos1 == slot, pos2 == slot), 1.0, 0.0).astype(jnp.bfloat16)
    pick = (mine_s * 512.0 + rank_s).astype(jnp.int32) - iota((pairs, cap), 1)

    for d in range(-1, 2):
        columns[p.xs(d)] = gat_b[1, p.xs(d)]
    for i in range(X_NEAR, len(X_PLAN)):
        x_hop(i, True).wait_recv()
    expand(start_ref, p.h * half, half, pick, lambda zz, xx: gat_a[1, zz, xx], lambda xx, zz: columns[xx, zz], own)

    @pl.loop(0, tiles)
    def _(j):
        acc[j] = jnp.dot(own[...], ints[:, span(j)], preferred_element_type=F32)

    @pl.loop(0, tiles)
    def _(j):
        ex_copy(j).wait_recv()
        total = acc[j] + jnp.dot(mix[...], recvb[j], preferred_element_type=F32)
        out_ref[:, span(j)] = total.astype(jnp.bfloat16)

    for i in range(X_NEAR, len(X_PLAN)):
        x_hop(i).wait_send()

    @pl.loop(0, tiles)
    def _(j):
        ex_copy(j).wait_send()


DMA = pltpu.SemaphoreType.DMA
VMEM_SPEC = pl.BlockSpec(memory_space=pltpu.VMEM)
ANY_SPEC = pl.BlockSpec(memory_space=pl.ANY)
SMEM_SPEC = pl.BlockSpec(memory_space=pltpu.SMEM)


def params(collective_id):
    return pltpu.CompilerParams(
        collective_id=collective_id, has_side_effects=True, vmem_limit_bytes=32 * 1024 * 1024
    )


def first(cap, slots, collective_id, starts, irreps, amp, integrals):
    rows, pairs = amp.shape
    depth, cols = integrals.shape
    bf16 = jnp.bfloat16
    shape = jax.ShapeDtypeStruct
    return pl.pallas_call(
        functools.partial(first_kernel, cap, slots),
        out_shape=(
            shape((slots, 2 * depth), bf16), shape((slots, 1), F32), shape((2 * depth, cols), bf16),
            shape((2, NZ, NX, PART, cap), bf16), shape((2, NX, NZ, rows - PART, cap), bf16),
            shape((4, 1, pairs), jnp.int32), shape((1,), jnp.int32),
        ),
        in_specs=[ANY_SPEC] * 4,
        out_specs=(VMEM_SPEC,) * 6 + (SMEM_SPEC,),
        scratch_shapes=[
            pltpu.VMEM((rows, cap), bf16),
            pltpu.SMEM(starts.shape, jnp.int32), pltpu.VMEM(irreps.shape, jnp.int32), pltpu.VMEM(amp.shape, bf16), DMA((3,)),
            DMA((3,)), DMA((3,)), DMA((2 * NX,)), DMA((2, NX)), DMA((2 * NZ,)), DMA((2, NZ)),
            DMA((2, len(Z_PLAN))), DMA((2, len(Z_PLAN))), DMA((2, len(X_PLAN))), DMA((2, len(X_PLAN))),
            DMA, DMA, DMA, pltpu.SemaphoreType.REGULAR,
        ],
        compiler_params=params(collective_id),
        name="gather_" + str(slots),
    )(starts, irreps, amp, integrals)


def second(cap, slots, collective_id, starts, lhs, low, ints, gat_a, gat_b, irr_all):
    pairs, cols, half = irr_all.shape[2], ints.shape[1], ints.shape[0]
    tiles = cols // TILE
    x_far = len(X_PLAN) - X_NEAR
    bf16 = jnp.bfloat16
    return pl.pallas_call(
        functools.partial(second_kernel, cap, slots),
        out_shape=jax.ShapeDtypeStruct((pairs, cols), bf16),
        in_specs=[ANY_SPEC] + [VMEM_SPEC] * 6,
        out_specs=VMEM_SPEC,
        scratch_shapes=[
            pltpu.SMEM(starts.shape, jnp.int32), DMA,
            pltpu.VMEM(gat_b.shape[1:], bf16),
            pltpu.VMEM((pairs, half), bf16),
            pltpu.VMEM((pairs, slots), bf16),
            pltpu.VMEM((tiles, pairs, TILE), F32),
            pltpu.VMEM((tiles, slots, TILE), bf16),
            pltpu.VMEM((tiles, slots, TILE), bf16),
            DMA((x_far,)), DMA((x_far,)), DMA((tiles,)), DMA((tiles,)),
        ],
        compiler_params=params(collective_id),
        name="exchange_" + str(slots),
    )(starts, lhs, low, ints, gat_a, gat_b, irr_all)


def per_device(amplitudes, integrals, irrep_start, pair_irrep):
    pairs = amplitudes.shape[0]
    operands = (irrep_start, pair_irrep, amplitudes.T, integrals)
    *state, size = first(CAP, SIZES[-1], 0, *operands)

    def full(state, operands):
        *state, _ = first(pairs, 2 * pairs, 1, *operands)
        return second(pairs, 2 * pairs, 2, operands[0], *state)

    def sized(slots, collective_id):
        return lambda state, operands: second(CAP, slots, collective_id, operands[0], *state)

    branches = [full] + [sized(slots, 3 + i) for i, slots in enumerate(reversed(SIZES))]
    return lax.switch(size[0], branches, state, operands)


def solution(mesh):
    placed = (P("pair", "col"), P("pair", "col"), P(), P("pair"))
    return jax.shard_map(
        per_device, mesh=mesh, in_specs=placed, out_specs=P("pair", "col"), check_vma=False
    )
```

```python
import functools

import jax
import jax.numpy as jnp
from jax import lax
from jax.experimental import pallas as pl
from jax.experimental.pallas import tpu as pltpu
from jax.sharding import PartitionSpec as P

MESH = pl.DeviceIdType.MESH
NX, NZ = 4, 8
TILE = 256
F32 = jnp.float32


def iota(shape, axis):
    return lax.broadcasted_iota(jnp.int32, shape, axis)


PART = 16
SIZES = (208, 256, 304, 352, 416, 448)
CAP = 128


class Place:
    def __init__(self):
        pair, col = lax.axis_index("pair"), lax.axis_index("col")
        self.pair, self.col = pair, col
        self.h, self.core = pair // 2, pair % 2
        self.yh, self.x, self.z = col // (NX * NZ), (col // NZ) % NX, col % NZ
        self.group = (1 - self.h) * 2 + self.core
        self.partner = self.at(1 - self.h, self.core, self.yh, self.x, self.z)
        self.sibling = self.at(self.h, 1 - self.core, self.yh, self.x, self.z)
        self.near = [self.along_x(d) for d in (1, -1)]

    def at(self, h, core, yh, x, z):
        return (h * 2 + core, (yh * NX + x) * NZ + z)

    def xs(self, d):
        return (self.x + NX + d) % NX

    def zs(self, d):
        return (self.z + NZ + d) % NZ

    def along_z(self, d):
        return self.at(self.h, self.core, self.yh, self.x, self.zs(d))

    def along_x(self, d):
        return self.at(self.h, self.core, self.yh, self.xs(d), self.z)


def remote(src, dst, send, recv, dev):
    return pltpu.make_async_remote_copy(
        src_ref=src, dst_ref=dst, send_sem=send, recv_sem=recv, device_id=dev, device_id_type=MESH
    )


def row_irrep(start_ref, row):
    total = jnp.int32(0)
    for j in range(1, 8):
        total = total + (row >= start_ref[j]).astype(jnp.int32)
    return total


def touch(start_ref, v, which, half):
    total = jnp.zeros_like(v)
    for r in range(8):
        meets = jnp.logical_and(start_ref[r] < half * (which + 1), start_ref[r + 1] > half * which)
        total = total + jnp.where(v == float(r), jnp.where(meets, 1.0, 0.0), 0.0)
    return total


def down(v):
    n = v.shape[1]
    return jnp.sum(jnp.where(iota((n, n), 0) == iota((n, n), 1), v, 0.0), axis=1, keepdims=True)


def expand(start_ref, first_row, half, keys, slab, column, dst):
    for b in range(half // 128):
        here = row_irrep(start_ref, first_row + b * 128) * 512
        one_hot = jnp.where(keys == here, 1.0, 0.0).astype(jnp.bfloat16)
        zz, xx = 2 * (b % (NZ // 2)), b // (NZ // 2)
        packed = jnp.concatenate([slab(zz, xx), column(xx, zz), slab(zz + 1, xx), column(xx, zz + 1)], axis=0)
        full = lax.dot_general(one_hot, packed, (((1,), (1,)), ((), ())), preferred_element_type=F32)
        dst[:, pl.ds(b * 128, 128)] = full.astype(jnp.bfloat16)


Z_PLAN = tuple((0, d, None) for d in (4, 3, -3, 2, -2, 1, -1))
X_PLAN = ((0, 1, 0), (0, -1, 1), (0, 1, 1), (0, -1, 0), (-1, 1, 0), (1, -1, 1))
X_NEAR = 4


def hop(place, axis, i, src, dst, send, recv, arriving=False):
    d, to, piece = (Z_PLAN if axis == "z" else X_PLAN)[i]
    index = place.zs if axis == "z" else place.xs
    n = (NX if axis == "z" else NZ) // 2

    def view(ref):
        ref = ref.at[index(d - to if arriving else d)]
        return ref if piece is None else ref.at[pl.ds(piece * n, n)]

    return remote(view(src), view(dst), send, recv, place.along_z(to) if axis == "z" else place.along_x(to))


def first_kernel(
    cap, slots,
    start_hbm, irr_hbm, amp_hbm, int_ref,
    lhs, low, ints, gat_a, gat_b, irr_all, size_ref,
    comp, start_ref, irr_ref, amp_ref, load_sem,
    irr_send, irr_recv, a_send, a_recv, b_send, b_recv, z_send, z_recv, x_send, x_recv,
    int_send, int_recv, own_sem, ready,
):
    p = Place()
    pairs = irr_ref.shape[0]
    depth, cols = int_ref.shape
    rows = amp_ref.shape[0]
    half = 2 * depth
    kind = (p.h == p.yh).astype(jnp.int32)
    selfish = p.h == p.yh

    loads = [
        pltpu.make_async_copy(src, dst, load_sem.at[i])
        for i, (src, dst) in enumerate(((irr_hbm, irr_ref), (start_hbm, start_ref), (amp_hbm, amp_ref)))
    ]
    for load in loads:
        load.start()

    barrier = pltpu.get_barrier_semaphore()

    def signal(dev, inc=1):
        pl.semaphore_signal(barrier, inc=inc, device_id=dev, device_id_type=MESH)

    for d in (4, 3, 5, 2, 6, 1, 7):
        for u in range(2):
            signal(p.at(u, p.core, p.h, p.x, p.zs(d)))
            if d < NX:
                signal(p.at(u, p.core, p.h, p.xs(d), p.z))
    for dev in [p.along_z(d) for _, d, _ in Z_PLAN] + p.near:
        signal(dev)
    for u in range(2):
        @pl.when(jnp.logical_not(jnp.logical_and(selfish, u == p.h)))
        def _(u=u):
            signal(p.at(u, p.core, p.h, p.x, p.z), 2)

    signal(p.partner)

    @pl.when(p.core == 0)
    def _():
        signal(p.sibling)

    own_copy = pltpu.make_async_copy(int_ref, ints.at[pl.ds(p.core * depth, depth)], own_sem)
    own_copy.start()
    for load in loads:
        load.wait()

    mine = irr_ref[...].reshape(1, pairs)
    irr_all[p.pair] = mine
    mine_l = mine.astype(F32)
    mine_s = down(mine_l)
    below = iota((pairs, pairs), 1) < iota((pairs, pairs), 0)
    rank_s = jnp.sum(jnp.where(jnp.logical_and(below, mine_s == mine_l), 1.0, 0.0), axis=1, keepdims=True)
    here = row_irrep(start_ref, p.col * rows).astype(F32)
    where_s = jnp.where(mine_s == here, rank_s, -1.0)
    chosen = jnp.where(where_s == iota((pairs, cap), 1).astype(F32), 1.0, 0.0).astype(jnp.bfloat16)
    block = jnp.dot(amp_ref[...], chosen, preferred_element_type=F32).astype(jnp.bfloat16)
    comp[...] = block

    @pl.when(selfish)
    def _():
        gat_a[1, p.z, p.x] = block[:PART]
        gat_b[1, p.x, p.z] = block[PART:]

    pl.semaphore_wait(barrier, 1 + len(p.near) + len(Z_PLAN) + 2 * (NX + NZ - kind) + p.core)

    comp_a, comp_b = comp.at[pl.ds(0, PART)], comp.at[pl.ds(PART, rows - PART)]

    def a_copy(u, d):
        dev = p.at(p.yh, p.core, u, p.xs(d), p.z)
        return remote(comp_a, gat_a.at[kind, p.z, p.x], a_send.at[u * NX + d], a_recv.at[kind, p.x], dev)

    def b_copy(u, d):
        dev = p.at(p.yh, p.core, u, p.x, p.zs(d))
        return remote(comp_b, gat_b.at[kind, p.x, p.z], b_send.at[u * NZ + d], b_recv.at[kind, p.z], dev)

    def first_hops(act):
        for d in (4, 3, 5, 2, 6, 1, 7):
            for u in range(2):
                act(b_copy(u, d))
                if d < NX:
                    act(a_copy(u, d))
        for u in range(2):
            @pl.when(jnp.logical_not(jnp.logical_and(selfish, u == p.yh)))
            def _(u=u):
                act(a_copy(u, 0))
                act(b_copy(u, 0))

    def irr_copy(k):
        g = p.pair if k < 2 else p.group
        dev = p.partner if k == 0 else p.sibling
        return remote(irr_all.at[g], irr_all.at[g], irr_send.at[k], irr_recv.at[k], dev)

    def irr_arrival(k):
        g = (p.group, p.h * 2 + 1 - p.core, (1 - p.h) * 2 + 1 - p.core)[k]
        return remote(irr_all.at[g], irr_all.at[g], irr_send.at[k], irr_recv.at[k], p.sibling)

    int_copy = remote(int_ref, ints.at[pl.ds(p.core * depth, depth)], int_send, int_recv, p.sibling)
    int_arrival = remote(int_ref, ints.at[pl.ds((1 - p.core) * depth, depth)], int_send, int_recv, p.sibling)

    irr_copy(0).start()
    first_hops(lambda c: c.start())

    @pl.when(p.core == 1)
    def _():
        pl.semaphore_signal(ready, inc=1, device_id=p.sibling, device_id_type=MESH)

    @pl.when(p.core == 0)
    def _():
        pl.semaphore_wait(ready, 1)

    int_copy.start()
    irr_copy(1).start()

    irr_arrival(0).wait_recv()
    irr_copy(2).start()

    def z_hop(t, i, arriving=False):
        return hop(p, "z", i, gat_a.at[t], gat_a.at[t], z_send.at[t, i], z_recv.at[t, i], arriving)

    def x_hop(t, i, arriving=False):
        return hop(p, "x", i, gat_b.at[t], gat_b.at[t], x_send.at[t, i], x_recv.at[t, i], arriving)

    def unless_own(t, d, act):
        if t == 1 and d == 0:
            @pl.when(jnp.logical_not(selfish))
            def _():
                act()
        else:
            act()

    def gather_start(t):
        for d in range(NZ):
            arrival = remote(comp_b, gat_b.at[t, p.x, p.zs(d)], b_send.at[0], b_recv.at[t, p.zs(d)], p.partner)
            unless_own(t, d, arrival.wait_recv)
        for i in range(X_NEAR):
            x_hop(t, i).start()
        for d in range(NX):
            arrival = remote(comp_a, gat_a.at[t, p.z, p.xs(d)], a_send.at[0], a_recv.at[t, p.xs(d)], p.partner)
            unless_own(t, d, arrival.wait_recv)
        for i in range(len(Z_PLAN)):
            z_hop(t, i).start()

    gather_start(0)
    for i in range(2):
        x_hop(0, i, True).wait_recv()
        x_hop(0, X_NEAR + i).start()
    gather_start(1)

    theirs_l = irr_all[p.group].astype(F32)
    theirs_s = down(theirs_l)
    above = iota((pairs, pairs), 0) < iota((pairs, pairs), 1)
    rank_l = jnp.sum(jnp.where(jnp.logical_and(above, theirs_s == theirs_l), 1.0, 0.0), axis=0, keepdims=True)
    key_l = theirs_l * 512.0 + rank_l + 1.0
    src_l = touch(start_ref, theirs_l, p.h, half)
    both_l = src_l * touch(start_ref, theirs_l, 1 - p.h, half)
    src_s, both_s = down(src_l), down(both_l)
    pos1 = jnp.sum(jnp.where(above, src_s, 0.0), axis=0, keepdims=True)
    pos2 = jnp.sum(src_l, axis=1, keepdims=True) + jnp.sum(jnp.where(above, both_s, 0.0), axis=0, keepdims=True)
    pos1 = jnp.where(src_l > 0.0, pos1, -1.0)
    pos2 = jnp.where(both_l > 0.0, pos2, -1.0)
    slot = iota((slots, pairs), 0).astype(F32)
    is_low = pos2 == slot
    key_slot = jnp.sum(jnp.where(jnp.logical_or(pos1 == slot, is_low), key_l, 0.0), axis=1, keepdims=True)
    low[...] = jnp.sum(jnp.where(is_low, 1.0, 0.0), axis=1, keepdims=True)
    pick = (key_slot - 1.0).astype(jnp.int32) - iota((slots, cap), 1)

    irr_arrival(1).wait_recv()
    irr_arrival(2).wait_recv()
    most = jnp.zeros((1, 1), F32)
    for g in range(4):
        v = irr_all[g].astype(F32)
        for r in range(8):
            count = jnp.sum(jnp.where(v == float(r), 1.0, 0.0), axis=1, keepdims=True)
            most = jnp.where(count > float(cap), 1e6, most)
        src = touch(start_ref, v, 1 - g // 2, half)
        need = jnp.sum(src + src * touch(start_ref, v, g // 2, half), axis=1, keepdims=True)
        most = jnp.maximum(most, need)
    choice = jnp.zeros((1, 1), F32)
    for size in SIZES:
        choice = choice + jnp.where(most <= float(size), 1.0, 0.0)
    size_ref[0] = jnp.sum(choice).astype(jnp.int32)

    for i in range(2, len(X_PLAN)):
        x_hop(0, i, True).wait_recv()
    for i in range(len(Z_PLAN)):
        z_hop(0, i, True).wait_recv()
    expand(
        start_ref, p.h * half, half, pick,
        lambda zz, xx: gat_a[0, zz, xx], lambda xx, zz: gat_b[0, xx, zz], lhs,
    )
    for i in range(X_NEAR):
        x_hop(1, i, True).wait_recv()
    for i in range(len(Z_PLAN)):
        z_hop(1, i, True).wait_recv()
    own_copy.wait()
    int_arrival.wait_recv()

    first_hops(lambda c: c.wait_send())
    for k in range(3):
        irr_copy(k).wait_send()
    int_copy.wait_send()
    for t in range(2):
        for i in range(len(Z_PLAN)):
            z_hop(t, i).wait_send()
        for i in range(X_NEAR if t else len(X_PLAN)):
            x_hop(t, i).wait_send()


def second_kernel(
    cap, slots,
    start_hbm, lhs, low, ints, gat_a, gat_b, irr_all,
    out_ref,
    start_ref, load_sem, columns, own, mix, acc, sendb, recvb,
    x_send, x_recv, ex_send, ex_recv,
):
    p = Place()
    pairs = irr_all.shape[2]
    half, cols = ints.shape
    tiles = cols // TILE

    barrier = pltpu.get_barrier_semaphore()
    for dev in p.near + [p.partner]:
        pl.semaphore_signal(barrier, inc=1, device_id=dev, device_id_type=MESH)
    load = pltpu.make_async_copy(start_hbm, start_ref, load_sem)
    load.start()

    def span(j):
        return pl.ds(pl.multiple_of(j * TILE, TILE), TILE)

    def product(j):
        full = jnp.dot(lhs[pl.ds(0, slots), :], ints[:, span(j)], preferred_element_type=F32)
        high = full.astype(jnp.bfloat16).astype(F32)
        sendb[j] = jnp.where(low[pl.ds(0, slots), :] > 0.0, full - high, full).astype(jnp.bfloat16)

    def ex_copy(j):
        return remote(sendb.at[j], recvb.at[j], ex_send.at[j], ex_recv.at[j], p.partner)

    product(0)
    pl.semaphore_wait(barrier, len(p.near) + 1)

    def x_hop(i, arriving=False):
        return hop(p, "x", i, gat_b.at[1], columns, x_send.at[i - X_NEAR], x_recv.at[i - X_NEAR], arriving)

    for i in range(X_NEAR, len(X_PLAN)):
        x_hop(i).start()

    load.wait()
    ex_copy(0).start()
    product(1)

    @pl.loop(2, tiles)
    def _(j):
        product(j)
        ex_copy(j - 1).start()

    mine_l = irr_all[p.pair].astype(F32)
    mine_s = down(mine_l)
    below = iota((pairs, pairs), 1) < iota((pairs, pairs), 0)
    rank_s = jnp.sum(jnp.where(jnp.logical_and(below, mine_s == mine_l), 1.0, 0.0), axis=1, keepdims=True)
    ex_copy(tiles - 1).start()
    src_l = touch(start_ref, mine_l, 1 - p.h, half)
    both_l = src_l * touch(start_ref, mine_l, p.h, half)
    src_s, both_s = down(src_l), down(both_l)
    pos1 = jnp.sum(jnp.where(below, src_l, 0.0), axis=1, keepdims=True)
    pos2 = jnp.sum(src_l, axis=1, keepdims=True) + jnp.sum(jnp.where(below, both_l, 0.0), axis=1, keepdims=True)
    pos1 = jnp.where(src_s > 0.0, pos1, -1.0)
    pos2 = jnp.where(both_s > 0.0, pos2, -1.0)
    slot = iota((pairs, slots), 1).astype(F32)
    mix[...] = jnp.where(jnp.logical_or(pos1 == slot, pos2 == slot), 1.0, 0.0).astype(jnp.bfloat16)
    pick = (mine_s * 512.0 + rank_s).astype(jnp.int32) - iota((pairs, cap), 1)

    for d in range(-1, 2):
        columns[p.xs(d)] = gat_b[1, p.xs(d)]
    for i in range(X_NEAR, len(X_PLAN)):
        x_hop(i, True).wait_recv()
    expand(start_ref, p.h * half, half, pick, lambda zz, xx: gat_a[1, zz, xx], lambda xx, zz: columns[xx, zz], own)

    @pl.loop(0, tiles)
    def _(j):
        acc[j] = jnp.dot(own[...], ints[:, span(j)], preferred_element_type=F32)

    @pl.loop(0, tiles)
    def _(j):
        ex_copy(j).wait_recv()
        total = acc[j] + jnp.dot(mix[...], recvb[j], preferred_element_type=F32)
        out_ref[:, span(j)] = total.astype(jnp.bfloat16)

    for i in range(X_NEAR, len(X_PLAN)):
        x_hop(i).wait_send()

    @pl.loop(0, tiles)
    def _(j):
        ex_copy(j).wait_send()


DMA = pltpu.SemaphoreType.DMA
VMEM_SPEC = pl.BlockSpec(memory_space=pltpu.VMEM)
ANY_SPEC = pl.BlockSpec(memory_space=pl.ANY)
SMEM_SPEC = pl.BlockSpec(memory_space=pltpu.SMEM)


def params(collective_id):
    return pltpu.CompilerParams(
        collective_id=collective_id, has_side_effects=True, vmem_limit_bytes=32 * 1024 * 1024
    )


def first(cap, slots, collective_id, starts, irreps, amp, integrals):
    rows, pairs = amp.shape
    depth, cols = integrals.shape
    bf16 = jnp.bfloat16
    shape = jax.ShapeDtypeStruct
    return pl.pallas_call(
        functools.partial(first_kernel, cap, slots),
        out_shape=(
            shape((slots, 2 * depth), bf16), shape((slots, 1), F32), shape((2 * depth, cols), bf16),
            shape((2, NZ, NX, PART, cap), bf16), shape((2, NX, NZ, rows - PART, cap), bf16),
            shape((4, 1, pairs), jnp.int32), shape((1,), jnp.int32),
        ),
        in_specs=[ANY_SPEC] * 4,
        out_specs=(VMEM_SPEC,) * 6 + (SMEM_SPEC,),
        scratch_shapes=[
            pltpu.VMEM((rows, cap), bf16),
            pltpu.SMEM(starts.shape, jnp.int32), pltpu.VMEM(irreps.shape, jnp.int32), pltpu.VMEM(amp.shape, bf16), DMA((3,)),
            DMA((3,)), DMA((3,)), DMA((2 * NX,)), DMA((2, NX)), DMA((2 * NZ,)), DMA((2, NZ)),
            DMA((2, len(Z_PLAN))), DMA((2, len(Z_PLAN))), DMA((2, len(X_PLAN))), DMA((2, len(X_PLAN))),
            DMA, DMA, DMA, pltpu.SemaphoreType.REGULAR,
        ],
        compiler_params=params(collective_id),
        name="gather_" + str(slots),
    )(starts, irreps, amp, integrals)


def second(cap, slots, collective_id, starts, lhs, low, ints, gat_a, gat_b, irr_all):
    pairs, cols, half = irr_all.shape[2], ints.shape[1], ints.shape[0]
    tiles = cols // TILE
    x_far = len(X_PLAN) - X_NEAR
    bf16 = jnp.bfloat16
    return pl.pallas_call(
        functools.partial(second_kernel, cap, slots),
        out_shape=jax.ShapeDtypeStruct((pairs, cols), bf16),
        in_specs=[ANY_SPEC] + [VMEM_SPEC] * 6,
        out_specs=VMEM_SPEC,
        scratch_shapes=[
            pltpu.SMEM(starts.shape, jnp.int32), DMA,
            pltpu.VMEM(gat_b.shape[1:], bf16),
            pltpu.VMEM((pairs, half), bf16),
            pltpu.VMEM((pairs, slots), bf16),
            pltpu.VMEM((tiles, pairs, TILE), F32),
            pltpu.VMEM((tiles, slots, TILE), bf16),
            pltpu.VMEM((tiles, slots, TILE), bf16),
            DMA((x_far,)), DMA((x_far,)), DMA((tiles,)), DMA((tiles,)),
        ],
        compiler_params=params(collective_id),
        name="exchange_" + str(slots),
    )(starts, lhs, low, ints, gat_a, gat_b, irr_all)


def per_device(amplitudes, integrals, irrep_start, pair_irrep):
    pairs = amplitudes.shape[0]
    operands = (irrep_start, pair_irrep, amplitudes.T, integrals)
    *state, size = first(CAP, SIZES[-1], 0, *operands)

    def full(state, operands):
        *state, _ = first(pairs, 2 * pairs, 1, *operands)
        return second(pairs, 2 * pairs, 2, operands[0], *state)

    def sized(slots, collective_id):
        return lambda state, operands: second(CAP, slots, collective_id, operands[0], *state)

    branches = [full] + [sized(slots, 3 + i) for i, slots in enumerate(reversed(SIZES))]
    return lax.switch(size[0], branches, state, operands)


def solution(mesh):
    placed = (P("pair", "col"), P("pair", "col"), P(), P("pair"))
    return jax.shard_map(
        per_device, mesh=mesh, in_specs=placed, out_specs=P("pair", "col"), check_vma=False
    )
```

```python
import functools

import jax
import jax.numpy as jnp
from jax import lax
from jax.experimental import pallas as pl
from jax.experimental.pallas import tpu as pltpu
from jax.sharding import PartitionSpec as P

MESH = pl.DeviceIdType.MESH
NX, NZ = 4, 8
TILE = 256
F32 = jnp.float32


def iota(shape, axis):
    return lax.broadcasted_iota(jnp.int32, shape, axis)


PART = 16
SIZES = (208, 256, 304, 352, 416, 448)
CAP = 128


class Place:
    def __init__(self):
        pair, col = lax.axis_index("pair"), lax.axis_index("col")
        self.pair, self.col = pair, col
        self.h, self.core = pair // 2, pair % 2
        self.yh, self.x, self.z = col // (NX * NZ), (col // NZ) % NX, col % NZ
        self.group = (1 - self.h) * 2 + self.core
        self.partner = self.at(1 - self.h, self.core, self.yh, self.x, self.z)
        self.sibling = self.at(self.h, 1 - self.core, self.yh, self.x, self.z)
        self.near = [self.along_x(d) for d in (1, -1)]

    def at(self, h, core, yh, x, z):
        return (h * 2 + core, (yh * NX + x) * NZ + z)

    def xs(self, d):
        return (self.x + NX + d) % NX

    def zs(self, d):
        return (self.z + NZ + d) % NZ

    def along_z(self, d):
        return self.at(self.h, self.core, self.yh, self.x, self.zs(d))

    def along_x(self, d):
        return self.at(self.h, self.core, self.yh, self.xs(d), self.z)


def remote(src, dst, send, recv, dev):
    return pltpu.make_async_remote_copy(
        src_ref=src, dst_ref=dst, send_sem=send, recv_sem=recv, device_id=dev, device_id_type=MESH
    )


def row_irrep(start_ref, row):
    total = jnp.int32(0)
    for j in range(1, 8):
        total = total + (row >= start_ref[j]).astype(jnp.int32)
    return total


def touch(start_ref, v, which, half):
    total = jnp.zeros_like(v)
    for r in range(8):
        meets = jnp.logical_and(start_ref[r] < half * (which + 1), start_ref[r + 1] > half * which)
        total = total + jnp.where(v == float(r), jnp.where(meets, 1.0, 0.0), 0.0)
    return total


def down(v):
    n = v.shape[1]
    return jnp.sum(jnp.where(iota((n, n), 0) == iota((n, n), 1), v, 0.0), axis=1, keepdims=True)


def expand(start_ref, first_row, half, keys, slab, column, dst, xx):
    for k in range(NZ // 2):
        b = xx * (NZ // 2) + k
        here = row_irrep(start_ref, first_row + b * 128) * 512
        one_hot = jnp.where(keys == here, 1.0, 0.0).astype(jnp.bfloat16)
        zz = 2 * k
        packed = jnp.concatenate([slab(zz, xx), column(xx, zz), slab(zz + 1, xx), column(xx, zz + 1)], axis=0)
        full = lax.dot_general(one_hot, packed, (((1,), (1,)), ((), ())), preferred_element_type=F32)
        dst[:, pl.ds(pl.multiple_of(b * 128, 128), 128)] = full.astype(jnp.bfloat16)


Z_PLAN = tuple((0, d, None) for d in (4, 3, -3, 2, -2, 1, -1))
X_PLAN = ((0, 1, 0), (0, -1, 1), (0, 1, 1), (0, -1, 0), (-1, 1, 0), (1, -1, 1))
X_NEAR = 4


def hop(place, axis, i, src, dst, send, recv, arriving=False):
    d, to, piece = (Z_PLAN if axis == "z" else X_PLAN)[i]
    index = place.zs if axis == "z" else place.xs
    n = (NX if axis == "z" else NZ) // 2

    def view(ref):
        ref = ref.at[index(d - to if arriving else d)]
        return ref if piece is None else ref.at[pl.ds(piece * n, n)]

    return remote(view(src), view(dst), send, recv, place.along_z(to) if axis == "z" else place.along_x(to))


def first_kernel(
    cap, slots,
    start_hbm, irr_hbm, amp_hbm, int_ref,
    lhs, low, ints, gat_a, gat_b, irr_all, size_ref,
    comp, start_ref, irr_ref, amp_ref, load_sem,
    irr_send, irr_recv, a_send, a_recv, b_send, b_recv, z_send, z_recv, x_send, x_recv,
    int_send, int_recv, own_sem, ready,
):
    p = Place()
    pairs = irr_ref.shape[0]
    depth, cols = int_ref.shape
    rows = amp_ref.shape[0]
    half = 2 * depth
    kind = (p.h == p.yh).astype(jnp.int32)
    selfish = p.h == p.yh

    loads = [
        pltpu.make_async_copy(src, dst, load_sem.at[i])
        for i, (src, dst) in enumerate(((irr_hbm, irr_ref), (start_hbm, start_ref), (amp_hbm, amp_ref)))
    ]
    for load in loads:
        load.start()

    barrier = pltpu.get_barrier_semaphore()

    def signal(dev, inc=1):
        pl.semaphore_signal(barrier, inc=inc, device_id=dev, device_id_type=MESH)

    for d in (4, 3, 5, 2, 6, 1, 7):
        for u in range(2):
            signal(p.at(u, p.core, p.h, p.x, p.zs(d)))
            if d < NX:
                signal(p.at(u, p.core, p.h, p.xs(d), p.z))
    for dev in [p.along_z(d) for _, d, _ in Z_PLAN] + p.near:
        signal(dev)
    for u in range(2):
        @pl.when(jnp.logical_not(jnp.logical_and(selfish, u == p.h)))
        def _(u=u):
            signal(p.at(u, p.core, p.h, p.x, p.z), 2)

    signal(p.partner)

    @pl.when(p.core == 0)
    def _():
        signal(p.sibling)

    own_copy = pltpu.make_async_copy(int_ref, ints.at[pl.ds(p.core * depth, depth)], own_sem)
    own_copy.start()
    for load in loads:
        load.wait()

    mine = irr_ref[...].reshape(1, pairs)
    irr_all[p.pair] = mine
    mine_l = mine.astype(F32)
    mine_s = down(mine_l)
    below = iota((pairs, pairs), 1) < iota((pairs, pairs), 0)
    rank_s = jnp.sum(jnp.where(jnp.logical_and(below, mine_s == mine_l), 1.0, 0.0), axis=1, keepdims=True)
    here = row_irrep(start_ref, p.col * rows).astype(F32)
    where_s = jnp.where(mine_s == here, rank_s, -1.0)
    chosen = jnp.where(where_s == iota((pairs, cap), 1).astype(F32), 1.0, 0.0).astype(jnp.bfloat16)
    block = jnp.dot(amp_ref[...], chosen, preferred_element_type=F32).astype(jnp.bfloat16)
    comp[...] = block

    @pl.when(selfish)
    def _():
        gat_a[1, p.z, p.x] = block[:PART]
        gat_b[1, p.x, p.z] = block[PART:]

    pl.semaphore_wait(barrier, 1 + len(p.near) + len(Z_PLAN) + 2 * (NX + NZ - kind) + p.core)

    comp_a, comp_b = comp.at[pl.ds(0, PART)], comp.at[pl.ds(PART, rows - PART)]

    def a_copy(u, d):
        dev = p.at(p.yh, p.core, u, p.xs(d), p.z)
        return remote(comp_a, gat_a.at[kind, p.z, p.x], a_send.at[u * NX + d], a_recv.at[kind, p.x], dev)

    def b_copy(u, d):
        dev = p.at(p.yh, p.core, u, p.x, p.zs(d))
        return remote(comp_b, gat_b.at[kind, p.x, p.z], b_send.at[u * NZ + d], b_recv.at[kind, p.z], dev)

    def first_hops(act):
        for d in (4, 3, 5, 2, 6, 1, 7):
            for u in range(2):
                act(b_copy(u, d))
                if d < NX:
                    act(a_copy(u, d))
        for u in range(2):
            @pl.when(jnp.logical_not(jnp.logical_and(selfish, u == p.yh)))
            def _(u=u):
                act(a_copy(u, 0))
                act(b_copy(u, 0))

    def irr_copy(k):
        g = p.pair if k < 2 else p.group
        dev = p.partner if k == 0 else p.sibling
        return remote(irr_all.at[g], irr_all.at[g], irr_send.at[k], irr_recv.at[k], dev)

    def irr_arrival(k):
        g = (p.group, p.h * 2 + 1 - p.core, (1 - p.h) * 2 + 1 - p.core)[k]
        return remote(irr_all.at[g], irr_all.at[g], irr_send.at[k], irr_recv.at[k], p.sibling)

    int_copy = remote(int_ref, ints.at[pl.ds(p.core * depth, depth)], int_send, int_recv, p.sibling)
    int_arrival = remote(int_ref, ints.at[pl.ds((1 - p.core) * depth, depth)], int_send, int_recv, p.sibling)

    irr_copy(0).start()
    first_hops(lambda c: c.start())

    @pl.when(p.core == 1)
    def _():
        pl.semaphore_signal(ready, inc=1, device_id=p.sibling, device_id_type=MESH)

    @pl.when(p.core == 0)
    def _():
        pl.semaphore_wait(ready, 1)

    int_copy.start()
    irr_copy(1).start()

    irr_arrival(0).wait_recv()
    irr_copy(2).start()

    def z_hop(t, i, arriving=False):
        return hop(p, "z", i, gat_a.at[t], gat_a.at[t], z_send.at[t, i], z_recv.at[t, i], arriving)

    def x_hop(t, i, arriving=False):
        return hop(p, "x", i, gat_b.at[t], gat_b.at[t], x_send.at[t, i], x_recv.at[t, i], arriving)

    def unless_own(t, d, act):
        if t == 1 and d == 0:
            @pl.when(jnp.logical_not(selfish))
            def _():
                act()
        else:
            act()

    def gather_start(t):
        for d in range(NZ):
            arrival = remote(comp_b, gat_b.at[t, p.x, p.zs(d)], b_send.at[0], b_recv.at[t, p.zs(d)], p.partner)
            unless_own(t, d, arrival.wait_recv)
        for i in range(X_NEAR):
            x_hop(t, i).start()
        for d in range(NX):
            arrival = remote(comp_a, gat_a.at[t, p.z, p.xs(d)], a_send.at[0], a_recv.at[t, p.xs(d)], p.partner)
            unless_own(t, d, arrival.wait_recv)
        for i in range(len(Z_PLAN)):
            z_hop(t, i).start()

    gather_start(0)
    for i in range(2):
        x_hop(0, i, True).wait_recv()
        x_hop(0, X_NEAR + i).start()
    gather_start(1)

    theirs_l = irr_all[p.group].astype(F32)
    theirs_s = down(theirs_l)
    above = iota((pairs, pairs), 0) < iota((pairs, pairs), 1)
    rank_l = jnp.sum(jnp.where(jnp.logical_and(above, theirs_s == theirs_l), 1.0, 0.0), axis=0, keepdims=True)
    key_l = theirs_l * 512.0 + rank_l + 1.0
    src_l = touch(start_ref, theirs_l, p.h, half)
    both_l = src_l * touch(start_ref, theirs_l, 1 - p.h, half)
    src_s, both_s = down(src_l), down(both_l)
    pos1 = jnp.sum(jnp.where(above, src_s, 0.0), axis=0, keepdims=True)
    pos2 = jnp.sum(src_l, axis=1, keepdims=True) + jnp.sum(jnp.where(above, both_s, 0.0), axis=0, keepdims=True)
    pos1 = jnp.where(src_l > 0.0, pos1, -1.0)
    pos2 = jnp.where(both_l > 0.0, pos2, -1.0)
    slot = iota((slots, pairs), 0).astype(F32)
    is_low = pos2 == slot
    key_slot = jnp.sum(jnp.where(jnp.logical_or(pos1 == slot, is_low), key_l, 0.0), axis=1, keepdims=True)
    low[...] = jnp.sum(jnp.where(is_low, 1.0, 0.0), axis=1, keepdims=True)
    pick = (key_slot - 1.0).astype(jnp.int32) - iota((slots, cap), 1)

    irr_arrival(1).wait_recv()
    irr_arrival(2).wait_recv()
    most = jnp.zeros((1, 1), F32)
    for g in range(4):
        v = irr_all[g].astype(F32)
        for r in range(8):
            count = jnp.sum(jnp.where(v == float(r), 1.0, 0.0), axis=1, keepdims=True)
            most = jnp.where(count > float(cap), 1e6, most)
        src = touch(start_ref, v, 1 - g // 2, half)
        need = jnp.sum(src + src * touch(start_ref, v, g // 2, half), axis=1, keepdims=True)
        most = jnp.maximum(most, need)
    choice = jnp.zeros((1, 1), F32)
    for size in SIZES:
        choice = choice + jnp.where(most <= float(size), 1.0, 0.0)
    size_ref[0] = jnp.sum(choice).astype(jnp.int32)

    def expand_column(d):
        expand(
            start_ref, p.h * half, half, pick,
            lambda zz, xx: gat_a[0, zz, xx], lambda xx, zz: gat_b[0, xx, zz], lhs, p.xs(d),
        )

    for i in range(len(Z_PLAN)):
        z_hop(0, i, True).wait_recv()
    expand_column(0)
    for i in range(2, X_NEAR):
        x_hop(0, i, True).wait_recv()
    expand_column(1)
    expand_column(-1)
    for i in range(X_NEAR, len(X_PLAN)):
        x_hop(0, i, True).wait_recv()
    expand_column(2)
    for i in range(X_NEAR):
        x_hop(1, i, True).wait_recv()
    for i in range(len(Z_PLAN)):
        z_hop(1, i, True).wait_recv()
    own_copy.wait()
    int_arrival.wait_recv()

    first_hops(lambda c: c.wait_send())
    for k in range(3):
        irr_copy(k).wait_send()
    int_copy.wait_send()
    for t in range(2):
        for i in range(len(Z_PLAN)):
            z_hop(t, i).wait_send()
        for i in range(X_NEAR if t else len(X_PLAN)):
            x_hop(t, i).wait_send()


def second_kernel(
    cap, slots,
    start_hbm, lhs, low, ints, gat_a, gat_b, irr_all,
    out_ref,
    start_ref, load_sem, columns, own, mix, acc, sendb, recvb,
    x_send, x_recv, ex_send, ex_recv,
):
    p = Place()
    pairs = irr_all.shape[2]
    half, cols = ints.shape
    tiles = cols // TILE

    barrier = pltpu.get_barrier_semaphore()
    for dev in p.near + [p.partner]:
        pl.semaphore_signal(barrier, inc=1, device_id=dev, device_id_type=MESH)
    load = pltpu.make_async_copy(start_hbm, start_ref, load_sem)
    load.start()

    def span(j):
        return pl.ds(pl.multiple_of(j * TILE, TILE), TILE)

    def product(j):
        full = jnp.dot(lhs[pl.ds(0, slots), :], ints[:, span(j)], preferred_element_type=F32)
        high = full.astype(jnp.bfloat16).astype(F32)
        sendb[j] = jnp.where(low[pl.ds(0, slots), :] > 0.0, full - high, full).astype(jnp.bfloat16)

    def ex_copy(j):
        return remote(sendb.at[j], recvb.at[j], ex_send.at[j], ex_recv.at[j], p.partner)

    product(0)
    pl.semaphore_wait(barrier, len(p.near) + 1)

    def x_hop(i, arriving=False):
        return hop(p, "x", i, gat_b.at[1], columns, x_send.at[i - X_NEAR], x_recv.at[i - X_NEAR], arriving)

    for i in range(X_NEAR, len(X_PLAN)):
        x_hop(i).start()

    load.wait()
    ex_copy(0).start()
    product(1)

    @pl.loop(2, tiles)
    def _(j):
        product(j)
        ex_copy(j - 1).start()

    mine_l = irr_all[p.pair].astype(F32)
    mine_s = down(mine_l)
    below = iota((pairs, pairs), 1) < iota((pairs, pairs), 0)
    rank_s = jnp.sum(jnp.where(jnp.logical_and(below, mine_s == mine_l), 1.0, 0.0), axis=1, keepdims=True)
    ex_copy(tiles - 1).start()
    src_l = touch(start_ref, mine_l, 1 - p.h, half)
    both_l = src_l * touch(start_ref, mine_l, p.h, half)
    src_s, both_s = down(src_l), down(both_l)
    pos1 = jnp.sum(jnp.where(below, src_l, 0.0), axis=1, keepdims=True)
    pos2 = jnp.sum(src_l, axis=1, keepdims=True) + jnp.sum(jnp.where(below, both_l, 0.0), axis=1, keepdims=True)
    pos1 = jnp.where(src_s > 0.0, pos1, -1.0)
    pos2 = jnp.where(both_s > 0.0, pos2, -1.0)
    slot = iota((pairs, slots), 1).astype(F32)
    mix[...] = jnp.where(jnp.logical_or(pos1 == slot, pos2 == slot), 1.0, 0.0).astype(jnp.bfloat16)
    pick = (mine_s * 512.0 + rank_s).astype(jnp.int32) - iota((pairs, cap), 1)

    for d in range(-1, 2):
        columns[p.xs(d)] = gat_b[1, p.xs(d)]
    for i in range(X_NEAR, len(X_PLAN)):
        x_hop(i, True).wait_recv()
    for xx in range(NX):
        expand(start_ref, p.h * half, half, pick, lambda zz, xx: gat_a[1, zz, xx], lambda xx, zz: columns[xx, zz], own, xx)

    @pl.loop(0, tiles)
    def _(j):
        acc[j] = jnp.dot(own[...], ints[:, span(j)], preferred_element_type=F32)

    @pl.loop(0, tiles)
    def _(j):
        ex_copy(j).wait_recv()
        total = acc[j] + jnp.dot(mix[...], recvb[j], preferred_element_type=F32)
        out_ref[:, span(j)] = total.astype(jnp.bfloat16)

    for i in range(X_NEAR, len(X_PLAN)):
        x_hop(i).wait_send()

    @pl.loop(0, tiles)
    def _(j):
        ex_copy(j).wait_send()


DMA = pltpu.SemaphoreType.DMA
VMEM_SPEC = pl.BlockSpec(memory_space=pltpu.VMEM)
ANY_SPEC = pl.BlockSpec(memory_space=pl.ANY)
SMEM_SPEC = pl.BlockSpec(memory_space=pltpu.SMEM)


def params(collective_id):
    return pltpu.CompilerParams(
        collective_id=collective_id, has_side_effects=True, vmem_limit_bytes=32 * 1024 * 1024
    )


def first(cap, slots, collective_id, starts, irreps, amp, integrals):
    rows, pairs = amp.shape
    depth, cols = integrals.shape
    bf16 = jnp.bfloat16
    shape = jax.ShapeDtypeStruct
    return pl.pallas_call(
        functools.partial(first_kernel, cap, slots),
        out_shape=(
            shape((slots, 2 * depth), bf16), shape((slots, 1), F32), shape((2 * depth, cols), bf16),
            shape((2, NZ, NX, PART, cap), bf16), shape((2, NX, NZ, rows - PART, cap), bf16),
            shape((4, 1, pairs), jnp.int32), shape((1,), jnp.int32),
        ),
        in_specs=[ANY_SPEC] * 4,
        out_specs=(VMEM_SPEC,) * 6 + (SMEM_SPEC,),
        scratch_shapes=[
            pltpu.VMEM((rows, cap), bf16),
            pltpu.SMEM(starts.shape, jnp.int32), pltpu.VMEM(irreps.shape, jnp.int32), pltpu.VMEM(amp.shape, bf16), DMA((3,)),
            DMA((3,)), DMA((3,)), DMA((2 * NX,)), DMA((2, NX)), DMA((2 * NZ,)), DMA((2, NZ)),
            DMA((2, len(Z_PLAN))), DMA((2, len(Z_PLAN))), DMA((2, len(X_PLAN))), DMA((2, len(X_PLAN))),
            DMA, DMA, DMA, pltpu.SemaphoreType.REGULAR,
        ],
        compiler_params=params(collective_id),
        name="gather_" + str(slots),
    )(starts, irreps, amp, integrals)


def second(cap, slots, collective_id, starts, lhs, low, ints, gat_a, gat_b, irr_all):
    pairs, cols, half = irr_all.shape[2], ints.shape[1], ints.shape[0]
    tiles = cols // TILE
    x_far = len(X_PLAN) - X_NEAR
    bf16 = jnp.bfloat16
    return pl.pallas_call(
        functools.partial(second_kernel, cap, slots),
        out_shape=jax.ShapeDtypeStruct((pairs, cols), bf16),
        in_specs=[ANY_SPEC] + [VMEM_SPEC] * 6,
        out_specs=VMEM_SPEC,
        scratch_shapes=[
            pltpu.SMEM(starts.shape, jnp.int32), DMA,
            pltpu.VMEM(gat_b.shape[1:], bf16),
            pltpu.VMEM((pairs, half), bf16),
            pltpu.VMEM((pairs, slots), bf16),
            pltpu.VMEM((tiles, pairs, TILE), F32),
            pltpu.VMEM((tiles, slots, TILE), bf16),
            pltpu.VMEM((tiles, slots, TILE), bf16),
            DMA((x_far,)), DMA((x_far,)), DMA((tiles,)), DMA((tiles,)),
        ],
        compiler_params=params(collective_id),
        name="exchange_" + str(slots),
    )(starts, lhs, low, ints, gat_a, gat_b, irr_all)


def per_device(amplitudes, integrals, irrep_start, pair_irrep):
    pairs = amplitudes.shape[0]
    operands = (irrep_start, pair_irrep, amplitudes.T, integrals)
    *state, size = first(CAP, SIZES[-1], 0, *operands)

    def full(state, operands):
        *state, _ = first(pairs, 2 * pairs, 1, *operands)
        return second(pairs, 2 * pairs, 2, operands[0], *state)

    def sized(slots, collective_id):
        return lambda state, operands: second(CAP, slots, collective_id, operands[0], *state)

    branches = [full] + [sized(slots, 3 + i) for i, slots in enumerate(reversed(SIZES))]
    return lax.switch(size[0], branches, state, operands)


def solution(mesh):
    placed = (P("pair", "col"), P("pair", "col"), P(), P("pair"))
    return jax.shard_map(
        per_device, mesh=mesh, in_specs=placed, out_specs=P("pair", "col"), check_vma=False
    )
```
